128 devices in a mesh: gx: 8 (over x, core), gy: 16 (over y, z).
Axes of the slice: x: 4, y: 4, z: 4, core: 2. Of those that a mesh axis runs over, the one named last changes fastest.
Arguments:
- point_coords: float32 [3, 2097152], P(None, ('gx', 'gy')), may hold values from -1 to 1
- strengths: float32 [3, 2097152], P(None, ('gx', 'gy')), may hold values from -0.06 to 0.06
- centers: float32 [3, 2048], replicated, may hold values from 0 to 0.3
- half_widths: float32 [2048], replicated, may hold values from 0.1 to 0.3
- tile_source: int32 [128, 128], P(('gx', 'gy')), may hold values from 0 to 2047, as said below
- tile_target: int32 [128, 128], P(('gx', 'gy')), may hold values from 0 to 2047, as said below
- tile_count: int32 [128], P(('gx', 'gy')), may hold values from 1 to 128, as said below
Outputs:
- velocity: float32 [3, 2097152], P(None, ('gx', 'gy'))
The draws below stay inside these ranges and needn't reach their ends.
Inputs may be any that keep to these rules, and one draw needn't show every extreme that they name: `tile_source`: cluster c belongs to domain c // 16. Among the first tile_count[d] entries of row d at most 1 name clusters of any one domain, and some domain reaches 1; later entries are valid ids of no interaction. `tile_target`: cluster c belongs to domain c // 16. Among the first tile_count[d] entries of row d at most 1 name clusters of any one domain, and some domain reaches 1; later entries are valid ids of no interaction. `tile_count`: 128 on at least one domain.
All inputs are finite; a program needn't handle non-finite values.
Results may differ from the reference program's by a relative error of at most 0.0001.
Values sent between devices are 32-bit elements; how exact they have to be, the bound alone decides.
No kernel may reach another device: no remote copies, remote signals or barrier semaphores. Data moves between devices by JAX's collectives and lax.ppermute only.
A program may use at most 64 MiB of HBM per device.

```python
import math
import jax
import jax.numpy as jnp
from jax import lax

CL_DEV = 16
PTS = 1024
DEG = 7
TILES_DEV = 128
Q = 512
DOMAINS = 128
CAP = 1
SLOTS = 128
CLUSTERS = 2048
POINTS = 2097152


def tile_tables(key):
    base_key = jax.random.fold_in(key, 4111)
    shift_key, fullest_key, source_key, target_key, source_local, target_local = jax.random.split(base_key, 6)
    shifts = jax.random.randint(shift_key, (DOMAINS,), 0, 4)
    totals = jnp.right_shift(jnp.full((DOMAINS,), TILES_DEV, jnp.int32), shifts)
    totals = jnp.maximum(totals, 1)
    fullest = jax.random.randint(fullest_key, (), 0, DOMAINS)
    totals = jnp.where(jnp.arange(DOMAINS) == fullest, TILES_DEV, totals).astype(jnp.int32)

    def owner_rows(owner_key):
        row_keys = jax.random.split(owner_key, DOMAINS)
        orders = jax.vmap(lambda row_key: jax.random.permutation(row_key, SLOTS))(row_keys)
        return orders[:, :TILES_DEV] // CAP
    sources = owner_rows(source_key) * CL_DEV + jax.random.randint(source_local, (DOMAINS, TILES_DEV), 0, CL_DEV)
    targets = owner_rows(target_key) * CL_DEV + jax.random.randint(target_local, (DOMAINS, TILES_DEV), 0, CL_DEV)
    return (sources.astype(jnp.int32), targets.astype(jnp.int32), totals)


def draw_tile_source(key, part):
    return tile_tables(key)[0]


def draw_tile_target(key, part):
    return tile_tables(key)[1]


def draw_tile_count(key, part):
    return tile_tables(key)[2]


def block_scale(own_key, dims, cuts, least, largest):
    level = 1.0
    for position, blocks in cuts:
        draws = jax.random.uniform(jax.random.fold_in(jax.random.fold_in(own_key, 6), position), (blocks,), jnp.float32, least / len(cuts), largest / len(cuts))
        level = level * jnp.repeat(jnp.exp(draws), dims[position] // blocks).reshape((-1,) + (1,) * (len(dims) - 1 - position))
    return level


def scatter_about(own_key, extent, deviation, reach, cuts=(), kind=jnp.bfloat16):
    array = jax.random.normal(own_key, extent, jnp.float32) * deviation
    if len(cuts) > 0:
        array = block_scale(own_key, extent, cuts, -0.22, 0.18) * array
    return jnp.clip(array, min=-reach, max=reach).astype(kind)


def setup_inputs(seed: int = 0) -> dict:
    streams_of = jax.random.split(jax.random.key(seed), 8)
    return {
        "point_coords": jnp.clip(jax.random.uniform(streams_of[0], (3, POINTS), jnp.float32, -1.0, 1.0) * block_scale(streams_of[0], (3, POINTS), ((1, 128),), -0.4, 0.0), -1.0, 1.0),
        "strengths": scatter_about(streams_of[1], (3, POINTS), 0.01, 0.06, ((1, 128),), jnp.float32),
        "centers": jnp.clip(jax.random.uniform(streams_of[2], (3, CLUSTERS), jnp.float32, 0.0, 0.3), 0.0, 0.3),
        "half_widths": jnp.clip(jnp.exp(jax.random.uniform(streams_of[3], (CLUSTERS,), jnp.float32, math.log(0.1), math.log(0.3))), 0.1, 0.3),
        "tile_source": draw_tile_source(jax.random.fold_in(streams_of[7], 71), 0),
        "tile_target": draw_tile_target(jax.random.fold_in(streams_of[7], 71), 0),
        "tile_count": draw_tile_count(jax.random.fold_in(streams_of[7], 71), 0),
    }


smoothing_sq = 0.01
biot_factor = -0.07957747154594767

def chebyshev(degree):
    counter = jnp.arange(degree + 1, dtype=jnp.float32)
    return jnp.cos(jnp.pi * counter / degree)

def lagrange(points, cheb_nodes):
    node_count = cheb_nodes.shape[0]
    differ = points[None, :] - cheb_nodes[:, None]
    diagonal = jnp.eye(node_count, dtype=bool)
    numerator = jnp.prod(jnp.where(diagonal[:, :, None], 1.0, differ[None, :, :]), axis=1)
    spacing = cheb_nodes[:, None] - cheb_nodes[None, :]
    denominator = jnp.prod(jnp.where(diagonal, 1.0, spacing), axis=1)
    return numerator / denominator[:, None]

def basis_parts(coords, cheb_nodes):
    basis_x = lagrange(coords[0], cheb_nodes)
    basis_y = lagrange(coords[1], cheb_nodes)
    basis_z = lagrange(coords[2], cheb_nodes)
    node_count = cheb_nodes.shape[0]
    paired = (basis_y[:, None, :] * basis_z[None, :, :]).reshape(node_count * node_count, -1)
    return (basis_x, paired)

def upward(coords, weights, cheb_nodes):
    basis_x, paired = basis_parts(coords, cheb_nodes)
    weighted = weights[:, None, :] * paired[None, :, :]
    charge = jnp.einsum('ai,cei->cae', basis_x, weighted, precision=lax.Precision.HIGHEST)
    return charge.reshape(3, -1)

def downward(coords, proxy_values, cheb_nodes):
    basis_x, paired = basis_parts(coords, cheb_nodes)
    node_count = cheb_nodes.shape[0]
    shaped = proxy_values.reshape(3, node_count, node_count * node_count)
    spread = jnp.einsum('cae,ai->cei', shaped, basis_x, precision=lax.Precision.HIGHEST)
    return lax.optimization_barrier(jnp.sum(spread * paired[None, :, :], axis=1))

def proxy_grid(center, half_width, cheb_nodes):
    node_count = cheb_nodes.shape[0]
    cube_shape = (node_count, node_count, node_count)
    along_x = jnp.broadcast_to(cheb_nodes[:, None, None], cube_shape).reshape(-1)
    along_y = jnp.broadcast_to(cheb_nodes[None, :, None], cube_shape).reshape(-1)
    along_z = jnp.broadcast_to(cheb_nodes[None, None, :], cube_shape).reshape(-1)
    return center[:, None] + half_width * jnp.stack([along_x, along_y, along_z])

def tile_velocity(target_grid, source_grid, charge):
    offset = target_grid[:, None, :] - source_grid[:, :, None]
    radius_sq = lax.optimization_barrier(jnp.sum(offset * offset, axis=0)) + smoothing_sq
    kernel = 1.0 / (radius_sq * jnp.sqrt(radius_sq))
    velocity_x = lax.optimization_barrier(jnp.sum(kernel * (offset[1] * charge[2][:, None] - offset[2] * charge[1][:, None]), axis=0))
    velocity_y = lax.optimization_barrier(jnp.sum(kernel * (offset[2] * charge[0][:, None] - offset[0] * charge[2][:, None]), axis=0))
    velocity_z = lax.optimization_barrier(jnp.sum(kernel * (offset[0] * charge[1][:, None] - offset[1] * charge[0][:, None]), axis=0))
    return biot_factor * jnp.stack([velocity_x, velocity_y, velocity_z])

def reference(point_coords, strengths, centers, half_widths, tile_source, tile_target, tile_count):
    cheb_nodes = chebyshev(DEG)
    coords = point_coords.reshape(3, CLUSTERS, PTS).transpose(1, 0, 2)
    weights = strengths.reshape(3, CLUSTERS, PTS).transpose(1, 0, 2)
    charges = lax.map(lambda pieces: upward(pieces[0], pieces[1], cheb_nodes), (coords, weights))
    proxy_grids = jax.vmap(lambda center, half_width: proxy_grid(center, half_width, cheb_nodes))(centers.T, half_widths)
    alive_mask = (jnp.arange(TILES_DEV)[None, :] < tile_count[:, None]).astype(jnp.float32).reshape(-1, 8)
    sources = tile_source.reshape(-1, 8)
    targets = tile_target.reshape(-1, 8)

    def add_group(totals, tile_group):
        source_ids, target_ids, alive_rows = tile_group
        contributions = jax.vmap(tile_velocity)(proxy_grids[target_ids], proxy_grids[source_ids], charges[source_ids])
        return (totals.at[target_ids].add(contributions * alive_rows[:, None, None]), None)
    empty_totals = jnp.zeros((CLUSTERS, 3, Q), jnp.float32)
    totals, _ = lax.scan(add_group, empty_totals, (sources, targets, alive_mask))
    velocity = lax.map(lambda pieces: downward(pieces[0], pieces[1], cheb_nodes), (coords, totals))
    return velocity.transpose(1, 0, 2).reshape(3, POINTS)
```

```python
import functools
import math

import jax
import jax.numpy as jnp
import numpy as np
from jax import lax
from jax.experimental import pallas as pl
from jax.experimental.pallas import tpu as pltpu
from jax.sharding import PartitionSpec as P

CL_DEV = 16
PTS = 1024
DEG = 7
TILES_DEV = 128
DOMAINS = 128
NODES = DEG + 1
AXES = ("gx", "gy")

smoothing_sq = 0.01
biot_factor = -0.07957747154594767

node_values = np.cos(np.pi * np.arange(NODES) / DEG)
node_list = [float(v) for v in node_values.astype(np.float32)]
node_scales = [
    1.0 / math.prod(node_list[a] - node_list[m] for m in range(NODES) if m != a)
    for a in range(NODES)
]


def build_constants():
    nodes = node_values.astype(np.float32)
    lane = np.arange(128)
    table = np.zeros((8, 8, 128), np.float32)
    for group in range(4):
        table[group] = nodes[group + 4 * (lane // 64)][None, :]
    table[4] = nodes[(lane // 8) % 8][None, :]
    table[5] = nodes[lane % 8][None, :]
    table[6] = nodes[:, None]
    table[7, :4] = table[:4, 0]
    return table


CONSTANTS = build_constants()


def split_bf16(value):
    high = value.astype(jnp.bfloat16)
    return high, (value - high.astype(jnp.float32)).astype(jnp.bfloat16)


def lagrange_rows(row, sublane):
    spread = jnp.broadcast_to(row, (NODES, row.shape[1]))
    result = None
    for m in range(NODES):
        factor = jnp.where(sublane == m, node_scales[m], spread - node_list[m])
        result = factor if result is None else result * factor
    return result


def paired_rows(basis_y, basis_z):
    return jnp.concatenate([basis_y[b : b + 1] * basis_z for b in range(NODES)], axis=0)


def upward_kernel(width_ref, coord_ref, strength_ref, const_ref, feature_ref, basis_ref, rows_ref):
    sublane = lax.broadcasted_iota(jnp.int32, (NODES, PTS), 0)
    lane = lax.broadcasted_iota(jnp.int32, (8, 128), 1)

    @pl.loop(0, CL_DEV)
    def _(cluster):
        start = pl.multiple_of(cluster * PTS, PTS)
        where = pl.ds(start, PTS)
        basis = [lagrange_rows(coord_ref[axis : axis + 1, where], sublane) for axis in range(3)]
        for axis in range(3):
            basis_ref[8 * axis : 8 * axis + 8, where] = basis[axis]
        paired = paired_rows(basis[1], basis[2])
        weighted = jnp.concatenate(
            [strength_ref[c : c + 1, where] * basis[0] for c in range(3)], axis=0
        )
        paired_high, paired_low = split_bf16(paired)
        weighted_high, weighted_low = split_bf16(weighted)
        left = jnp.concatenate([weighted_high, weighted_low], axis=0)
        contract = functools.partial(
            lax.dot_general,
            dimension_numbers=(((1,), (1,)), ((), ())),
            preferred_element_type=jnp.float32,
        )
        twice_high = jnp.concatenate([paired_high, paired_high], axis=0)
        twice_low = jnp.concatenate([paired_low, paired_low], axis=0)
        by_high = contract(left, twice_high)
        by_low = contract(weighted_high, twice_low)
        charge = by_high[:24] + by_high[24:] + by_low
        charge = charge * biot_factor
        charges = []
        for c in range(3):
            block = charge[8 * c : 8 * c + 8]
            moved = jnp.concatenate([block[4:], block[:4]], axis=0)
            charges.append(jnp.where(lane < 64, block, moved))
        width = width_ref[cluster]
        node_x = const_ref[7] * width
        node_y = const_ref[4] * width
        node_z = const_ref[5] * width
        moments = [
            node_y * charges[2] - node_z * charges[1],
            node_z * charges[0] - node_x * charges[2],
            node_x * charges[1] - node_y * charges[0],
        ]
        order = [charges[0], charges[1], charges[2], charges[0], charges[1]] + moments
        for row, value in enumerate(order):
            for group in range(4):
                rows_ref[row : row + 1, 128 * group : 128 * group + 128] = value[group : group + 1]
        high, low = split_bf16(rows_ref[...])
        feature_ref[cluster] = jnp.concatenate([high, low], axis=0)


def tile_kernel(domain_ref, request_ref, center_ref, width_ref, feature_ref, const_ref, out_ref, order_ref, high_ref, low_ref):
    sublane = lax.broadcasted_iota(jnp.int32, (8, 128), 0)

    def collect(peer, count):
        order_ref[count] = peer
        return count + (request_ref[peer, 0, 0] > 0).astype(jnp.int32)

    total = lax.fori_loop(0, DOMAINS, collect, 0)
    domain = domain_ref[0]

    @pl.loop(0, total)
    def _(step):
        peer = order_ref[step]
        local_id = request_ref[peer, 0, 0] - 1
        source = domain * CL_DEV + local_id
        target = request_ref[peer, 0, 1]
        source_width = width_ref[source]
        target_width = width_ref[target]
        shift = [center_ref[axis, target] - center_ref[axis, source] for axis in range(3)]
        target_x = [const_ref[group] * target_width + shift[0] for group in range(4)]
        target_y = const_ref[4] * target_width + shift[1]
        target_z = const_ref[5] * target_width + shift[2]
        apart_z = target_z - const_ref[6] * source_width
        square_z = apart_z * apart_z + smoothing_sq
        square_yz = []
        for b in range(NODES):
            apart_y = target_y - source_width * node_list[b]
            square_yz.append(square_z + apart_y * apart_y)
        for group in range(4):
            for half in range(2):
                source_x = source_width * node_list[group + 4 * half]
                for lanes in range(4):
                    apart_x = target_x[lanes] - source_x
                    square_x = apart_x * apart_x
                    for b in range(0, NODES, 2):
                        pair = []
                        for part in range(2):
                            inverse = lax.rsqrt(square_yz[b + part] + square_x)
                            pair.append(inverse * inverse * inverse)
                        kernel = jnp.concatenate(pair, axis=0)
                        high, low = split_bf16(kernel)
                        first = group * 128 + half * 64 + b * 8
                        place = (slice(first, first + 16), slice(128 * lanes, 128 * lanes + 128))
                        high_ref[place] = high
                        low_ref[place] = low
        feature = feature_ref[local_id]
        summed = jnp.dot(feature, high_ref[...], preferred_element_type=jnp.float32)
        summed += jnp.dot(feature, low_ref[...], preferred_element_type=jnp.float32)
        summed = summed[:8] + summed[8:]
        for lanes in range(4):
            block = summed[:, 128 * lanes : 128 * lanes + 128]
            first = jnp.where(sublane == 0, target_y, jnp.where(sublane == 1, target_z, target_x[lanes]))
            second = jnp.where(sublane == 0, target_z, jnp.where(sublane == 1, target_x[lanes], target_y))
            velocity = (
                first * pltpu.roll(block, 6, 0)
                - second * pltpu.roll(block, 7, 0)
                - pltpu.roll(block, 3, 0)
            )
            for c in range(3):
                out_ref[peer * 12 + c * 4 + lanes] = velocity[c : c + 1]


def relay_kernel(order_ref, in_ref, out_ref):
    @pl.loop(0, DOMAINS, step=4)
    def _(first):
        for extra in range(4):
            peer = first + extra
            place = order_ref[peer]
            rows = in_ref[pl.ds(jnp.maximum(place, 0) * 12, 12)]
            out_ref[pl.ds(peer * 12, 12)] = jnp.where(place < 0, 0.0, rows)


def downward_kernel(owner_ref, part_ref, basis_ref, out_ref, proxy_ref):
    cluster_row = lax.broadcasted_iota(jnp.int32, (CL_DEV, DOMAINS), 0)
    assign = (owner_ref[...] == cluster_row + 1).astype(jnp.bfloat16)
    for chunk in range(12):
        high, low = split_bf16(part_ref[pl.ds(chunk, DOMAINS, stride=12), :])
        proxy_ref[chunk * CL_DEV : (chunk + 1) * CL_DEV] = jnp.dot(
            assign, high, preferred_element_type=jnp.float32
        ) + jnp.dot(assign, low, preferred_element_type=jnp.float32)

    @pl.loop(0, CL_DEV)
    def _(cluster):
        start = pl.multiple_of(cluster * PTS, PTS)
        where = pl.ds(start, PTS)
        rows = proxy_ref[pl.ds(cluster, 12, stride=CL_DEV), :]
        near, far = rows[:, :64], rows[:, 64:]
        left = jnp.concatenate(
            [piece[4 * c : 4 * c + 4] for c in range(3) for piece in (near, far)], axis=0
        )
        left_high, left_low = split_bf16(left)
        paired = paired_rows(basis_ref[8:16, where], basis_ref[16:24, where])
        paired_high, paired_low = split_bf16(paired)
        spread = jnp.dot(
            jnp.concatenate([left_high, left_low], axis=0),
            paired_high,
            preferred_element_type=jnp.float32,
        )
        spread = spread[:24] + spread[24:] + jnp.dot(
            left_high, paired_low, preferred_element_type=jnp.float32
        )
        basis_x = basis_ref[0:8, where]
        for c in range(3):
            out_ref[c : c + 1, where] = jnp.sum(
                spread[8 * c : 8 * c + 8] * basis_x, axis=0, keepdims=True
            )


def in_vmem():
    return pl.BlockSpec(memory_space=pltpu.VMEM)


def in_smem():
    return pl.BlockSpec(memory_space=pltpu.SMEM)


def exchange(value):
    return lax.all_to_all(value, AXES, split_axis=0, concat_axis=0, tiled=True)


def local(point_coords, strengths, centers, half_widths, tile_source, tile_target, tile_count):
    domain = lax.axis_index(AXES)
    const = jnp.asarray(CONSTANTS)
    source_ids = tile_source[0]
    target_ids = tile_target[0]
    alive = jnp.arange(TILES_DEV) < tile_count[0]
    slots = jnp.arange(DOMAINS)[:, None]
    from_source = (slots == (source_ids // CL_DEV)[None, :]) & alive[None, :]
    from_target = (slots == (target_ids // CL_DEV)[None, :]) & alive[None, :]
    source_code = jnp.sum(
        jnp.where(from_source, (target_ids * 32 + source_ids % CL_DEV + 1)[None, :], 0), axis=1
    )
    target_code = jnp.sum(
        jnp.where(
            from_target, ((source_ids // CL_DEV) * 32 + target_ids % CL_DEV + 1)[None, :], 0
        ),
        axis=1,
    )
    message = jnp.stack([source_code % 32, source_code // 32, target_code % 32], axis=1)
    relay_order = jnp.where(target_code > 0, target_code // 32, -1)
    received = exchange(message.reshape(DOMAINS, 1, 3))

    own_widths = lax.dynamic_slice_in_dim(half_widths, domain * CL_DEV, CL_DEV)
    features, basis = pl.pallas_call(
        upward_kernel,
        out_shape=(
            jax.ShapeDtypeStruct((CL_DEV, 16, 512), jnp.bfloat16),
            jax.ShapeDtypeStruct((24, CL_DEV * PTS), jnp.float32),
        ),
        in_specs=[in_smem(), in_vmem(), in_vmem(), in_vmem()],
        out_specs=(in_vmem(), in_vmem()),
        scratch_shapes=[pltpu.VMEM((8, 512), jnp.float32)],
        cost_estimate=pl.CostEstimate(flops=10**8, bytes_accessed=2 * 10**6, transcendentals=0),
        name="upward",
    )(own_widths, point_coords, strengths, const)

    parts = pl.pallas_call(
        tile_kernel,
        out_shape=jax.ShapeDtypeStruct((DOMAINS * 12, 1, 128), jnp.float32),
        in_specs=[in_smem(), in_smem(), in_smem(), in_smem(), in_vmem(), in_vmem()],
        out_specs=in_vmem(),
        scratch_shapes=[
            pltpu.SMEM((DOMAINS,), jnp.int32),
            pltpu.VMEM((512, 512), jnp.bfloat16),
            pltpu.VMEM((512, 512), jnp.bfloat16),
        ],
        name="tiles",
    )(domain.reshape(1), received, centers, half_widths, features, const)

    relayed = exchange(parts.reshape(DOMAINS, 1, 1536))
    ordered = pl.pallas_call(
        relay_kernel,
        out_shape=jax.ShapeDtypeStruct((DOMAINS * 12, 1, 128), jnp.float32),
        in_specs=[in_smem(), in_vmem()],
        out_specs=in_vmem(),
        name="relay",
    )(relay_order, relayed.reshape(DOMAINS * 12, 1, 128))
    arrived = exchange(ordered.reshape(DOMAINS, 1, 1536))

    owners = received[:, 0, 2]
    return pl.pallas_call(
        downward_kernel,
        out_shape=jax.ShapeDtypeStruct((3, CL_DEV * PTS), jnp.float32),
        in_specs=[in_vmem(), in_vmem(), in_vmem()],
        out_specs=in_vmem(),
        scratch_shapes=[pltpu.VMEM((12 * CL_DEV, 128), jnp.float32)],
        name="downward",
    )(owners.reshape(1, DOMAINS), arrived.reshape(DOMAINS * 12, 128), basis)


def solution(mesh):
    return jax.shard_map(
        local,
        mesh=mesh,
        in_specs=(
            P(None, AXES),
            P(None, AXES),
            P(),
            P(),
            P(AXES, None),
            P(AXES, None),
            P(AXES),
        ),
        out_specs=P(None, AXES),
        check_vma=False,
    )
```

```python
import functools
import math

import jax
import jax.numpy as jnp
import numpy as np
from jax import lax
from jax.experimental import pallas as pl
from jax.experimental.pallas import tpu as pltpu
from jax.sharding import PartitionSpec as P

CL_DEV = 16
PTS = 1024
DEG = 7
TILES_DEV = 128
DOMAINS = 128
NODES = DEG + 1
GROUP = 4
AXES = ("gx", "gy")

smoothing_sq = 0.01
biot_factor = -0.07957747154594767

node_values = np.cos(np.pi * np.arange(NODES) / DEG)
node_list = [float(v) for v in node_values.astype(np.float32)]
node_scales = [
    1.0 / math.prod(node_list[a] - node_list[m] for m in range(NODES) if m != a)
    for a in range(NODES)
]


def build_constants():
    nodes = node_values.astype(np.float32)
    lane = np.arange(128)
    table = np.zeros((8, 8, 128), np.float32)
    for group in range(4):
        table[group] = nodes[group + 4 * (lane // 64)][None, :]
    table[4] = nodes[(lane // 8) % 8][None, :]
    table[5] = nodes[lane % 8][None, :]
    table[6] = nodes[:, None]
    table[7, :4] = table[:4, 0]
    return table


CONSTANTS = build_constants()


def split_bf16(value):
    high = value.astype(jnp.bfloat16)
    return high, (value - high.astype(jnp.float32)).astype(jnp.bfloat16)


def lagrange_rows(row, sublane):
    spread = jnp.broadcast_to(row, (NODES, row.shape[1]))
    result = None
    for m in range(NODES):
        factor = jnp.where(sublane == m, node_scales[m], spread - node_list[m])
        result = factor if result is None else result * factor
    return result


def paired_rows(basis_y, basis_z):
    return jnp.concatenate([basis_y[b : b + 1] * basis_z for b in range(NODES)], axis=0)


def message_kernel(count_ref, source_ref, target_ref, out_ref):
    slot = lax.broadcasted_iota(jnp.int32, (DOMAINS, TILES_DEV), 0)
    lane = lax.broadcasted_iota(jnp.int32, (DOMAINS, TILES_DEV), 1)
    alive = lane < count_ref[0]
    source = source_ref[...]
    target = target_ref[...]
    from_source = (slot == source // CL_DEV) & alive
    from_target = (slot == target // CL_DEV) & alive
    source_code = jnp.sum(
        jnp.where(from_source, target * 32 + source % CL_DEV + 1, 0), axis=1, keepdims=True
    )
    target_local = jnp.sum(
        jnp.where(from_target, target % CL_DEV + 1, 0), axis=1, keepdims=True
    )
    out_ref[...] = jnp.where(
        lane == 0,
        source_code % 32,
        jnp.where(lane == 1, source_code // 32, jnp.where(lane == 2, target_local, 0)),
    )


def basis_kernel(coord_ref, basis_ref):
    sublane = lax.broadcasted_iota(jnp.int32, (NODES, PTS), 0)

    @pl.loop(0, CL_DEV)
    def _(cluster):
        where = pl.ds(pl.multiple_of(cluster * PTS, PTS), PTS)
        for axis in range(3):
            basis_ref[8 * axis : 8 * axis + 8, where] = lagrange_rows(
                coord_ref[axis : axis + 1, where], sublane
            )


def upward_kernel(domain_ref, width_ref, coord_ref, strength_ref, const_ref, center_ref, all_width_ref, feature_ref, place_ref, same_ref, rows_ref):
    same_ref[...] = const_ref[...]
    place_ref[0:3] = center_ref[...]
    place_ref[3:4] = all_width_ref[...]
    sublane = lax.broadcasted_iota(jnp.int32, (NODES, PTS), 0)
    lane = lax.broadcasted_iota(jnp.int32, (8, 128), 1)

    def one_cluster(cluster, rows):
        where = pl.ds(pl.multiple_of(cluster * PTS, PTS), PTS)
        basis = [lagrange_rows(coord_ref[axis : axis + 1, where], sublane) for axis in range(3)]
        paired = paired_rows(basis[1], basis[2])
        weighted = jnp.concatenate(
            [strength_ref[c : c + 1, where] * basis[0] for c in range(3)], axis=0
        )
        paired_high, paired_low = split_bf16(paired)
        weighted_high, weighted_low = split_bf16(weighted)
        left = jnp.concatenate([weighted_high, weighted_low], axis=0)
        contract = functools.partial(
            lax.dot_general,
            dimension_numbers=(((1,), (1,)), ((), ())),
            preferred_element_type=jnp.float32,
        )
        twice_high = jnp.concatenate([paired_high, paired_high], axis=0)
        twice_low = jnp.concatenate([paired_low, paired_low], axis=0)
        by_high = contract(left, twice_high)
        by_low = contract(weighted_high, twice_low)
        charge = by_high[:24] + by_high[24:] + by_low
        charge = charge * biot_factor
        charges = []
        for c in range(3):
            block = charge[8 * c : 8 * c + 8]
            moved = jnp.concatenate([block[4:], block[:4]], axis=0)
            charges.append(jnp.where(lane < 64, block, moved))
        width = width_ref[domain_ref[0] * CL_DEV + cluster]
        node_x = const_ref[7] * width
        node_y = const_ref[4] * width
        node_z = const_ref[5] * width
        moments = [
            node_y * charges[2] - node_z * charges[1],
            node_z * charges[0] - node_x * charges[2],
            node_x * charges[1] - node_y * charges[0],
        ]
        order = [charges[0], charges[1], charges[2], charges[0], charges[1]] + moments
        for row, value in enumerate(order):
            for group in range(4):
                rows[row : row + 1, 128 * group : 128 * group + 128] = value[group : group + 1]
        high, low = split_bf16(rows[...])
        feature_ref[cluster] = jnp.concatenate([high, low], axis=0)

    @pl.loop(0, CL_DEV, step=2)
    def _(cluster):
        for extra in range(2):
            one_cluster(cluster + extra, rows_ref.at[extra])


def kernel_blocks(width, target_x, square_yz, group_pair, lane_pair):
    highs, lows = [], []
    for lanes in (2 * lane_pair, 2 * lane_pair + 1):
        high_rows, low_rows = [], []
        for group in (2 * group_pair, 2 * group_pair + 1):
            for half in range(2):
                apart_x = target_x[lanes] - width * node_list[group + 4 * half]
                square_x = apart_x * apart_x
                for b in range(0, NODES, 2):
                    pair = []
                    for square in square_yz[b : b + 2]:
                        inverse = lax.rsqrt(square + square_x)
                        pair.append(inverse * inverse * inverse)
                    high, low = split_bf16(jnp.concatenate(pair, axis=0))
                    high_rows.append(high)
                    low_rows.append(low)
        highs.append(jnp.concatenate(high_rows, axis=0))
        lows.append(jnp.concatenate(low_rows, axis=0))
    return jnp.concatenate(highs, axis=1), jnp.concatenate(lows, axis=1)


def tile_kernel(domain_ref, request_ref, place_ref, feature_ref, const_ref, out_ref, order_ref):
    sublane = lax.broadcasted_iota(jnp.int32, (8, 128), 0)

    def collect(peer, count):
        order_ref[count] = peer
        return count + (request_ref[peer, 0, 0] > 0).astype(jnp.int32)

    total = lax.fori_loop(0, DOMAINS, collect, 0)
    last = order_ref[jnp.maximum(total - 1, 0)]
    for extra in range(GROUP - 1):
        order_ref[total + extra] = last
    domain = domain_ref[0]

    def one_tile(peer):
        local_id = request_ref[peer, 0, 0] - 1
        source = domain * CL_DEV + local_id
        target = request_ref[peer, 0, 1]
        source_width = place_ref[3, source]
        target_width = place_ref[3, target]
        shift = [place_ref[axis, target] - place_ref[axis, source] for axis in range(3)]
        target_x = [const_ref[group] * target_width + shift[0] for group in range(4)]
        target_y = const_ref[4] * target_width + shift[1]
        target_z = const_ref[5] * target_width + shift[2]
        apart_z = target_z - const_ref[6] * source_width
        square_z = apart_z * apart_z + smoothing_sq
        square_yz = []
        for b in range(NODES):
            apart_y = target_y - source_width * node_list[b]
            square_yz.append(square_z + apart_y * apart_y)
        feature = feature_ref[local_id]
        for lane_pair in range(2):
            summed = None
            for group_pair in range(2):
                columns = feature[:, 256 * group_pair : 256 * group_pair + 256]
                for block in kernel_blocks(
                    source_width, target_x, square_yz, group_pair, lane_pair
                ):
                    product = jnp.dot(columns, block, preferred_element_type=jnp.float32)
                    summed = product if summed is None else summed + product
            summed = summed[:8] + summed[8:]
            for side in range(2):
                lanes = 2 * lane_pair + side
                block = summed[:, 128 * side : 128 * side + 128]
                first = jnp.where(
                    sublane == 0, target_y, jnp.where(sublane == 1, target_z, target_x[lanes])
                )
                second = jnp.where(
                    sublane == 0, target_z, jnp.where(sublane == 1, target_x[lanes], target_y)
                )
                velocity = (
                    first * pltpu.roll(block, 6, 0)
                    - second * pltpu.roll(block, 7, 0)
                    - pltpu.roll(block, 3, 0)
                )
                for c in range(3):
                    out_ref[peer * 12 + c * 4 + lanes] = velocity[c : c + 1]

    @pl.loop(0, (total + GROUP - 1) // GROUP)
    def _(step):
        for extra in range(GROUP):
            one_tile(order_ref[step * GROUP + extra])


def relay_kernel(order_ref, in_ref, out_ref, semaphore):
    @pl.loop(0, DOMAINS, step=8)
    def _(first):
        for extra in range(8):
            peer = first + extra
            pltpu.make_async_copy(
                in_ref.at[pl.ds(order_ref[peer] * 12, 12)],
                out_ref.at[pl.ds(peer * 12, 12)],
                semaphore,
            ).start()

    pltpu.make_async_copy(in_ref, out_ref, semaphore).wait()


def downward_kernel(owner_ref, part_ref, basis_ref, out_ref, proxy_ref):
    owner = owner_ref[...]
    column = lax.broadcasted_iota(jnp.int32, (DOMAINS, CL_DEV), 1)
    assign = (owner == column + 1).astype(jnp.bfloat16)
    alive = jnp.broadcast_to(owner > 0, (DOMAINS, 128))
    gather = functools.partial(
        lax.dot_general,
        dimension_numbers=(((0,), (0,)), ((), ())),
        preferred_element_type=jnp.float32,
    )
    for chunk in range(12):
        part = jnp.where(alive, part_ref[pl.ds(chunk, DOMAINS, stride=12), :], 0.0)
        high, low = split_bf16(part)
        proxy_ref[chunk * CL_DEV : (chunk + 1) * CL_DEV] = gather(assign, high) + gather(
            assign, low
        )

    def one_cluster(cluster):
        where = pl.ds(pl.multiple_of(cluster * PTS, PTS), PTS)
        rows = proxy_ref[pl.ds(cluster, 12, stride=CL_DEV), :]
        near, far = rows[:, :64], rows[:, 64:]
        left = jnp.concatenate(
            [piece[4 * c : 4 * c + 4] for c in range(3) for piece in (near, far)], axis=0
        )
        left_high, left_low = split_bf16(left)
        paired_high, paired_low = split_bf16(
            paired_rows(basis_ref[8:16, where], basis_ref[16:24, where])
        )
        spread = jnp.dot(
            jnp.concatenate([left_high, left_low, left_high], axis=1),
            jnp.concatenate([paired_high, paired_high, paired_low], axis=0),
            preferred_element_type=jnp.float32,
        )
        basis_x = basis_ref[0:8, where]
        for c in range(3):
            out_ref[c : c + 1, where] = jnp.sum(
                spread[8 * c : 8 * c + 8] * basis_x, axis=0, keepdims=True
            )

    @pl.loop(0, CL_DEV, step=2)
    def _(cluster):
        one_cluster(cluster)
        one_cluster(cluster + 1)


def in_vmem():
    return pl.BlockSpec(memory_space=pltpu.VMEM)


def in_smem():
    return pl.BlockSpec(memory_space=pltpu.SMEM)


def exchange(value):
    return lax.all_to_all(value, AXES, split_axis=0, concat_axis=0, tiled=True)


def settings(mebibytes):
    return pltpu.CompilerParams(vmem_limit_bytes=mebibytes << 20)


def local(point_coords, strengths, centers, half_widths, tile_source, tile_target, tile_count):
    domain = lax.axis_index(AXES).reshape(1)
    const = jnp.asarray(CONSTANTS)
    message = pl.pallas_call(
        message_kernel,
        out_shape=jax.ShapeDtypeStruct((DOMAINS, 128), jnp.int32),
        in_specs=[in_smem(), in_vmem(), in_vmem()],
        out_specs=in_vmem(),
        name="message",
    )(tile_count, tile_source, tile_target)
    received = exchange(message.reshape(DOMAINS, 1, 128))

    features, places, kept_const = pl.pallas_call(
        upward_kernel,
        out_shape=(
            jax.ShapeDtypeStruct((CL_DEV, 16, 512), jnp.bfloat16),
            jax.ShapeDtypeStruct((4, centers.shape[1]), jnp.float32),
            jax.ShapeDtypeStruct(const.shape, jnp.float32),
        ),
        in_specs=[in_smem(), in_smem()] + [in_vmem()] * 5,
        out_specs=(in_vmem(), in_vmem(), in_vmem()),
        scratch_shapes=[pltpu.VMEM((2, 8, 512), jnp.float32)],
        compiler_params=settings(8),
        cost_estimate=pl.CostEstimate(flops=10**8, bytes_accessed=10**6, transcendentals=0),
        name="upward",
    )(domain, half_widths, point_coords, strengths, const, centers, half_widths[None, :])

    parts = pl.pallas_call(
        tile_kernel,
        out_shape=jax.ShapeDtypeStruct((DOMAINS * 12, 1, 128), jnp.float32),
        in_specs=[in_smem(), in_smem(), in_smem(), in_vmem(), in_vmem()],
        out_specs=in_vmem(),
        scratch_shapes=[pltpu.SMEM((DOMAINS + GROUP,), jnp.int32)],
        compiler_params=settings(8),
        name="tiles",
    )(domain, received, places, features, kept_const)

    relayed = exchange(parts.reshape(DOMAINS, 1, 1536))
    alive = jnp.arange(TILES_DEV) < tile_count[0]
    from_target = (jnp.arange(DOMAINS)[:, None] == (tile_target[0] // CL_DEV)[None, :]) & alive
    relay_order = jnp.sum(jnp.where(from_target, (tile_source[0] // CL_DEV)[None, :], 0), axis=1)
    ordered = pl.pallas_call(
        relay_kernel,
        out_shape=jax.ShapeDtypeStruct((DOMAINS * 12, 1, 128), jnp.float32),
        in_specs=[in_smem(), in_vmem()],
        out_specs=pl.BlockSpec(memory_space=pl.ANY),
        scratch_shapes=[pltpu.SemaphoreType.DMA],
        compiler_params=settings(4),
        name="relay",
    )(relay_order, relayed.reshape(DOMAINS * 12, 1, 128))
    arrived = exchange(ordered.reshape(DOMAINS, 1, 1536))

    basis = pl.pallas_call(
        basis_kernel,
        out_shape=jax.ShapeDtypeStruct((24, CL_DEV * PTS), jnp.float32),
        in_specs=[in_vmem()],
        out_specs=in_vmem(),
        compiler_params=settings(8),
        cost_estimate=pl.CostEstimate(flops=10**8, bytes_accessed=2 * 10**6, transcendentals=0),
        name="basis",
    )(point_coords)
    owners = received[:, 0, 2:3]
    return pl.pallas_call(
        downward_kernel,
        out_shape=jax.ShapeDtypeStruct((3, CL_DEV * PTS), jnp.float32),
        in_specs=[in_vmem(), in_vmem(), in_vmem()],
        out_specs=in_vmem(),
        scratch_shapes=[pltpu.VMEM((12 * CL_DEV, 128), jnp.float32)],
        compiler_params=settings(8),
        name="downward",
    )(owners, arrived.reshape(DOMAINS * 12, 128), basis)


def solution(mesh):
    return jax.shard_map(
        local,
        mesh=mesh,
        in_specs=(
            P(None, AXES),
            P(None, AXES),
            P(),
            P(),
            P(AXES, None),
            P(AXES, None),
            P(AXES),
        ),
        out_specs=P(None, AXES),
        check_vma=False,
    )
```

```python
import functools
import math

import jax
import jax.numpy as jnp
import numpy as np
from jax import lax
from jax.experimental import pallas as pl
from jax.experimental.pallas import tpu as pltpu
from jax.sharding import PartitionSpec as P

CL_DEV = 16
PTS = 1024
DEG = 7
TILES_DEV = 128
DOMAINS = 128
NODES = DEG + 1
GROUP = 4
AXES = ("gx", "gy")

smoothing_sq = 0.01
biot_factor = -0.07957747154594767

node_values = np.cos(np.pi * np.arange(NODES) / DEG)
node_list = [float(v) for v in node_values.astype(np.float32)]
node_scales = [
    1.0 / math.prod(node_list[a] - node_list[m] for m in range(NODES) if m != a)
    for a in range(NODES)
]


def build_constants():
    nodes = node_values.astype(np.float32)
    lane = np.arange(128)
    table = np.zeros((8, 8, 128), np.float32)
    for group in range(4):
        table[group] = nodes[group + 4 * (lane // 64)][None, :]
    table[4] = nodes[(lane // 8) % 8][None, :]
    table[5] = nodes[lane % 8][None, :]
    table[6] = nodes[:, None]
    table[7, :4] = table[:4, 0]
    return table


CONSTANTS = build_constants()


def split_bf16(value):
    high = value.astype(jnp.bfloat16)
    return high, (value - high.astype(jnp.float32)).astype(jnp.bfloat16)


def lagrange_rows(row, sublane):
    spread = jnp.broadcast_to(row, (NODES, row.shape[1]))
    result = None
    for m in range(NODES):
        factor = jnp.where(sublane == m, node_scales[m], spread - node_list[m])
        result = factor if result is None else result * factor
    return result


def paired_rows(basis_y, basis_z):
    return jnp.concatenate([basis_y[b : b + 1] * basis_z for b in range(NODES)], axis=0)


def split_exactly(value):
    high = value.astype(jnp.bfloat16)
    rest = value - high.astype(jnp.float32)
    middle = rest.astype(jnp.bfloat16)
    return high, middle, (rest - middle.astype(jnp.float32)).astype(jnp.bfloat16)


def message_kernel(count_ref, source_ref, target_ref, center_ref, width_ref, out_ref):
    slot = lax.broadcasted_iota(jnp.int32, (DOMAINS, TILES_DEV), 0)
    lane = lax.broadcasted_iota(jnp.int32, (1, TILES_DEV), 1)
    alive = lane < count_ref[0]
    source = jnp.where(alive, source_ref[...], -1)
    target = jnp.where(alive, target_ref[...], -1)
    from_source = jnp.where(slot == source >> 4, 1.0, 0.0).astype(jnp.bfloat16)
    from_target = jnp.where(slot == target >> 4, 1.0, 0.0).astype(jnp.bfloat16)
    clusters = center_ref.shape[1]
    number = lax.broadcasted_iota(jnp.int32, (clusters, TILES_DEV), 0)
    chosen = jnp.where(number == target, 1.0, 0.0).astype(jnp.bfloat16)
    places = jnp.concatenate([center_ref[...], width_ref[...], jnp.zeros((4, clusters))], axis=0)
    terms = jnp.concatenate(split_exactly(places), axis=0)
    rows = jnp.dot(terms, chosen, preferred_element_type=jnp.float32)
    row = lax.broadcasted_iota(jnp.int32, (24, TILES_DEV), 0)
    local_source = ((source & 15) + 1).astype(jnp.float32)
    local_target = ((target & 15) + 1).astype(jnp.float32)
    rows = jnp.where(row == 4, local_source, rows)
    spread = functools.partial(
        lax.dot_general,
        dimension_numbers=(((1,), (1,)), ((), ())),
        preferred_element_type=jnp.float32,
    )
    out_ref[:, 0:24] = spread(from_source, rows.astype(jnp.bfloat16)) + spread(
        from_target, jnp.where(row == 5, local_target, 0.0).astype(jnp.bfloat16)
    )


def basis_kernel(coord_ref, basis_ref):
    sublane = lax.broadcasted_iota(jnp.int32, (NODES, PTS), 0)

    @pl.loop(0, CL_DEV)
    def _(cluster):
        where = pl.ds(pl.multiple_of(cluster * PTS, PTS), PTS)
        for axis in range(3):
            basis_ref[8 * axis : 8 * axis + 8, where] = lagrange_rows(
                coord_ref[axis : axis + 1, where], sublane
            )


def upward_kernel(domain_ref, width_ref, coord_ref, strength_ref, const_ref, center_ref, all_width_ref, feature_ref, own_ref, same_ref, rows_ref):
    same_ref[...] = const_ref[...]
    domain = domain_ref[0]
    nearby = pl.ds(pl.multiple_of((domain >> 3) * 128, 128), 128)
    places = jnp.concatenate(
        [center_ref[:, nearby], all_width_ref[:, nearby], jnp.zeros((4, 128))], axis=0
    )
    own_ref[...] = pltpu.roll(places, 128 - (domain & 7) * CL_DEV, 1)
    sublane = lax.broadcasted_iota(jnp.int32, (NODES, PTS), 0)
    lane = lax.broadcasted_iota(jnp.int32, (8, 128), 1)

    def one_cluster(cluster, rows):
        where = pl.ds(pl.multiple_of(cluster * PTS, PTS), PTS)
        basis = [lagrange_rows(coord_ref[axis : axis + 1, where], sublane) for axis in range(3)]
        paired = paired_rows(basis[1], basis[2])
        weighted = jnp.concatenate(
            [strength_ref[c : c + 1, where] * basis[0] for c in range(3)], axis=0
        )
        paired_high, paired_low = split_bf16(paired)
        weighted_high, weighted_low = split_bf16(weighted)
        left = jnp.concatenate([weighted_high, weighted_low], axis=0)
        contract = functools.partial(
            lax.dot_general,
            dimension_numbers=(((1,), (1,)), ((), ())),
            preferred_element_type=jnp.float32,
        )
        twice_high = jnp.concatenate([paired_high, paired_high], axis=0)
        twice_low = jnp.concatenate([paired_low, paired_low], axis=0)
        by_high = contract(left, twice_high)
        by_low = contract(weighted_high, twice_low)
        charge = by_high[:24] + by_high[24:] + by_low
        charge = charge * biot_factor
        charges = []
        for c in range(3):
            block = charge[8 * c : 8 * c + 8]
            moved = jnp.concatenate([block[4:], block[:4]], axis=0)
            charges.append(jnp.where(lane < 64, block, moved))
        width = width_ref[domain * CL_DEV + cluster]
        node_x = const_ref[7] * width
        node_y = const_ref[4] * width
        node_z = const_ref[5] * width
        moments = [
            node_y * charges[2] - node_z * charges[1],
            node_z * charges[0] - node_x * charges[2],
            node_x * charges[1] - node_y * charges[0],
        ]
        order = [charges[0], charges[1], charges[2], charges[0], charges[1]] + moments
        for row, value in enumerate(order):
            for group in range(4):
                rows[row : row + 1, 128 * group : 128 * group + 128] = value[group : group + 1]
        high, low = split_bf16(rows[...])
        feature_ref[cluster] = jnp.concatenate([high, low], axis=0)

    @pl.loop(0, CL_DEV, step=2)
    def _(cluster):
        for extra in range(2):
            one_cluster(cluster + extra, rows_ref.at[extra])


def kernel_blocks(width, target_x, square_yz, group_pair, lane_pair):
    highs, lows = [], []
    for lanes in (2 * lane_pair, 2 * lane_pair + 1):
        high_rows, low_rows = [], []
        for group in (2 * group_pair, 2 * group_pair + 1):
            for half in range(2):
                apart_x = target_x[lanes] - width * node_list[group + 4 * half]
                square_x = apart_x * apart_x
                for b in range(0, NODES, 2):
                    pair = []
                    for square in square_yz[b : b + 2]:
                        inverse = lax.rsqrt(square + square_x)
                        pair.append(inverse * inverse * inverse)
                    high, low = split_bf16(jnp.concatenate(pair, axis=0))
                    high_rows.append(high)
                    low_rows.append(low)
        highs.append(jnp.concatenate(high_rows, axis=0))
        lows.append(jnp.concatenate(low_rows, axis=0))
    return jnp.concatenate(highs, axis=1), jnp.concatenate(lows, axis=1)


def tile_kernel(request_ref, own_ref, feature_ref, const_ref, out_ref, order_ref, number_ref, place_ref, number_vmem, place_vmem, semaphore):
    sublane = lax.broadcasted_iota(jnp.int32, (8, 128), 0)
    request = request_ref[...].T
    request = request[0:8] + request[8:16] + request[16:24]
    number_vmem[...] = request.astype(jnp.int32)
    place_vmem[0:8] = request
    place_vmem[8:16] = own_ref[...]
    copies = [
        pltpu.make_async_copy(number_vmem, number_ref, semaphore.at[0]),
        pltpu.make_async_copy(place_vmem, place_ref, semaphore.at[1]),
    ]
    for copy in copies:
        copy.start()
    for copy in copies:
        copy.wait()

    def collect(step, count):
        for extra in range(8):
            peer = step * 8 + extra
            order_ref[count] = peer
            count += (number_ref[4, peer] > 0).astype(jnp.int32)
        return count

    total = lax.fori_loop(0, DOMAINS // 8, collect, 0)
    last = order_ref[jnp.maximum(total - 1, 0)]
    for extra in range(GROUP - 1):
        order_ref[total + extra] = last

    def one_tile(peer):
        local_id = number_ref[4, peer] - 1
        source_width = place_ref[11, local_id]
        target_width = place_ref[3, peer]
        shift = [place_ref[axis, peer] - place_ref[8 + axis, local_id] for axis in range(3)]
        target_x = [const_ref[group] * target_width + shift[0] for group in range(4)]
        target_y = const_ref[4] * target_width + shift[1]
        target_z = const_ref[5] * target_width + shift[2]
        apart_z = target_z - const_ref[6] * source_width
        square_z = apart_z * apart_z + smoothing_sq
        square_yz = []
        for b in range(NODES):
            apart_y = target_y - source_width * node_list[b]
            square_yz.append(square_z + apart_y * apart_y)
        feature = feature_ref[local_id]
        for lane_pair in range(2):
            summed = None
            for group_pair in range(2):
                columns = feature[:, 256 * group_pair : 256 * group_pair + 256]
                for block in kernel_blocks(
                    source_width, target_x, square_yz, group_pair, lane_pair
                ):
                    product = jnp.dot(columns, block, preferred_element_type=jnp.float32)
                    summed = product if summed is None else summed + product
            summed = summed[:8] + summed[8:]
            for side in range(2):
                lanes = 2 * lane_pair + side
                block = summed[:, 128 * side : 128 * side + 128]
                first = jnp.where(
                    sublane == 0, target_y, jnp.where(sublane == 1, target_z, target_x[lanes])
                )
                second = jnp.where(
                    sublane == 0, target_z, jnp.where(sublane == 1, target_x[lanes], target_y)
                )
                velocity = (
                    first * pltpu.roll(block, 6, 0)
                    - second * pltpu.roll(block, 7, 0)
                    - pltpu.roll(block, 3, 0)
                )
                for c in range(3):
                    out_ref[peer * 12 + c * 4 + lanes] = velocity[c : c + 1]

    @pl.loop(0, (total + GROUP - 1) // GROUP)
    def _(step):
        for extra in range(GROUP):
            one_tile(order_ref[step * GROUP + extra])


def relay_kernel(order_ref, in_ref, out_ref, semaphore):
    @pl.loop(0, DOMAINS, step=8)
    def _(first):
        for extra in range(8):
            peer = first + extra
            pltpu.make_async_copy(
                in_ref.at[pl.ds(order_ref[peer] * 12, 12)],
                out_ref.at[pl.ds(peer * 12, 12)],
                semaphore,
            ).start()

    pltpu.make_async_copy(in_ref, out_ref, semaphore).wait()


def downward_kernel(owner_ref, part_ref, basis_ref, out_ref, proxy_ref):
    owner = owner_ref[:, 5:6].astype(jnp.int32)
    column = lax.broadcasted_iota(jnp.int32, (DOMAINS, CL_DEV), 1)
    assign = (owner == column + 1).astype(jnp.bfloat16)
    alive = jnp.broadcast_to(owner > 0, (DOMAINS, 128))
    gather = functools.partial(
        lax.dot_general,
        dimension_numbers=(((0,), (0,)), ((), ())),
        preferred_element_type=jnp.float32,
    )
    for chunk in range(12):
        part = jnp.where(alive, part_ref[pl.ds(chunk, DOMAINS, stride=12), :], 0.0)
        high, low = split_bf16(part)
        proxy_ref[chunk * CL_DEV : (chunk + 1) * CL_DEV] = gather(assign, high) + gather(
            assign, low
        )

    def one_cluster(cluster):
        where = pl.ds(cluster * PTS, PTS)
        rows = proxy_ref[pl.ds(cluster, 12, stride=CL_DEV), :]
        near, far = rows[:, :64], rows[:, 64:]
        left = jnp.concatenate(
            [piece[4 * c : 4 * c + 4] for c in range(3) for piece in (near, far)], axis=0
        )
        left_high, left_low = split_bf16(left)
        paired_high, paired_low = split_bf16(
            paired_rows(basis_ref[8:16, where], basis_ref[16:24, where])
        )
        spread = jnp.dot(
            jnp.concatenate([left_high, left_low, left_high], axis=1),
            jnp.concatenate([paired_high, paired_high, paired_low], axis=0),
            preferred_element_type=jnp.float32,
        )
        basis_x = basis_ref[0:8, where]
        for c in range(3):
            out_ref[c : c + 1, where] = jnp.sum(
                spread[8 * c : 8 * c + 8] * basis_x, axis=0, keepdims=True
            )

    for cluster in range(CL_DEV):
        one_cluster(cluster)


def in_vmem():
    return pl.BlockSpec(memory_space=pltpu.VMEM)


def in_smem():
    return pl.BlockSpec(memory_space=pltpu.SMEM)


def exchange(value):
    return lax.all_to_all(value, AXES, split_axis=0, concat_axis=0, tiled=True)


def settings(mebibytes):
    return pltpu.CompilerParams(vmem_limit_bytes=mebibytes << 20)


def local(point_coords, strengths, centers, half_widths, tile_source, tile_target, tile_count):
    domain = lax.axis_index(AXES).reshape(1)
    const = jnp.asarray(CONSTANTS)
    message = pl.pallas_call(
        message_kernel,
        out_shape=jax.ShapeDtypeStruct((DOMAINS, 128), jnp.float32),
        in_specs=[in_smem()] + [in_vmem()] * 4,
        out_specs=in_vmem(),
        name="message",
    )(tile_count, tile_source, tile_target, centers, half_widths[None, :])
    received = exchange(message.reshape(DOMAINS, 1, 128)).reshape(DOMAINS, 128)

    features, own_places, kept_const = pl.pallas_call(
        upward_kernel,
        out_shape=(
            jax.ShapeDtypeStruct((CL_DEV, 16, 512), jnp.bfloat16),
            jax.ShapeDtypeStruct((8, 128), jnp.float32),
            jax.ShapeDtypeStruct(const.shape, jnp.float32),
        ),
        in_specs=[in_smem(), in_smem()] + [in_vmem()] * 5,
        out_specs=(in_vmem(), in_vmem(), in_vmem()),
        scratch_shapes=[pltpu.VMEM((2, 8, 512), jnp.float32)],
        compiler_params=settings(8),
        cost_estimate=pl.CostEstimate(flops=10**8, bytes_accessed=10**6, transcendentals=0),
        name="upward",
    )(domain, half_widths, point_coords, strengths, const, centers, half_widths[None, :])

    parts = pl.pallas_call(
        tile_kernel,
        out_shape=jax.ShapeDtypeStruct((DOMAINS * 12, 1, 128), jnp.float32),
        in_specs=[in_vmem()] * 4,
        out_specs=in_vmem(),
        scratch_shapes=[
            pltpu.SMEM((DOMAINS + GROUP,), jnp.int32),
            pltpu.SMEM((8, 128), jnp.int32),
            pltpu.SMEM((16, 128), jnp.float32),
            pltpu.VMEM((8, 128), jnp.int32),
            pltpu.VMEM((16, 128), jnp.float32),
            pltpu.SemaphoreType.DMA((2,)),
        ],
        compiler_params=settings(8),
        name="tiles",
    )(received, own_places, features, kept_const)

    relayed = exchange(parts.reshape(DOMAINS, 1, 1536))
    alive = jnp.arange(TILES_DEV) < tile_count[0]
    from_target = (jnp.arange(DOMAINS)[:, None] == (tile_target[0] // CL_DEV)[None, :]) & alive
    relay_order = jnp.sum(jnp.where(from_target, (tile_source[0] // CL_DEV)[None, :], 0), axis=1)
    ordered = pl.pallas_call(
        relay_kernel,
        out_shape=jax.ShapeDtypeStruct((DOMAINS * 12, 1, 128), jnp.float32),
        in_specs=[in_smem(), in_vmem()],
        out_specs=pl.BlockSpec(memory_space=pl.ANY),
        scratch_shapes=[pltpu.SemaphoreType.DMA],
        compiler_params=settings(4),
        name="relay",
    )(relay_order, relayed.reshape(DOMAINS * 12, 1, 128))
    arrived = exchange(ordered.reshape(DOMAINS, 1, 1536))

    basis = pl.pallas_call(
        basis_kernel,
        out_shape=jax.ShapeDtypeStruct((24, CL_DEV * PTS), jnp.float32),
        in_specs=[in_vmem()],
        out_specs=in_vmem(),
        compiler_params=settings(8),
        cost_estimate=pl.CostEstimate(flops=10**8, bytes_accessed=2 * 10**6, transcendentals=0),
        name="basis",
    )(point_coords)
    return pl.pallas_call(
        downward_kernel,
        out_shape=jax.ShapeDtypeStruct((3, CL_DEV * PTS), jnp.float32),
        in_specs=[in_vmem(), in_vmem(), in_vmem()],
        out_specs=in_vmem(),
        scratch_shapes=[pltpu.VMEM((12 * CL_DEV, 128), jnp.float32)],
        compiler_params=settings(8),
        name="downward",
    )(received, arrived.reshape(DOMAINS * 12, 128), basis)


def solution(mesh):
    return jax.shard_map(
        local,
        mesh=mesh,
        in_specs=(
            P(None, AXES),
            P(None, AXES),
            P(),
            P(),
            P(AXES, None),
            P(AXES, None),
            P(AXES),
        ),
        out_specs=P(None, AXES),
        check_vma=False,
    )
```

```python
import functools
import math

import jax
import jax.numpy as jnp
import numpy as np
from jax import lax
from jax.experimental import pallas as pl
from jax.experimental.pallas import tpu as pltpu
from jax.sharding import PartitionSpec as P

CL_DEV = 16
PTS = 1024
DEG = 7
TILES_DEV = 128
DOMAINS = 128
NODES = DEG + 1
WIDE = 8
NARROW = 4
AXES = ("gx", "gy")

smoothing_sq = 0.01
biot_factor = -0.07957747154594767

node_values = np.cos(np.pi * np.arange(NODES) / DEG)
node_list = [float(v) for v in node_values.astype(np.float32)]
node_scales = [
    1.0 / math.prod(node_list[a] - node_list[m] for m in range(NODES) if m != a)
    for a in range(NODES)
]


def build_constants():
    nodes = node_values.astype(np.float32)
    lane = np.arange(128)
    table = np.zeros((8, 8, 128), np.float32)
    for group in range(4):
        table[group] = nodes[group + 4 * (lane // 64)][None, :]
    table[4] = nodes[(lane // 8) % 8][None, :]
    table[5] = nodes[lane % 8][None, :]
    table[6] = nodes[:, None]
    table[7, :4] = table[:4, 0]
    return table


CONSTANTS = build_constants()


def split_bf16(value):
    high = value.astype(jnp.bfloat16)
    return high, (value - high.astype(jnp.float32)).astype(jnp.bfloat16)


def lagrange_rows(row, sublane):
    spread = jnp.broadcast_to(row, (NODES, row.shape[1]))
    result = None
    for m in range(NODES):
        factor = jnp.where(sublane == m, node_scales[m], spread - node_list[m])
        result = factor if result is None else result * factor
    return result


def paired_rows(basis_y, basis_z):
    return jnp.concatenate([basis_y[b : b + 1] * basis_z for b in range(NODES)], axis=0)


def split_exactly(value):
    high = value.astype(jnp.bfloat16)
    rest = value - high.astype(jnp.float32)
    middle = rest.astype(jnp.bfloat16)
    return high, middle, (rest - middle.astype(jnp.float32)).astype(jnp.bfloat16)


def message_kernel(count_ref, source_ref, target_ref, center_ref, width_ref, out_ref):
    slot = lax.broadcasted_iota(jnp.int32, (DOMAINS, TILES_DEV), 0)
    lane = lax.broadcasted_iota(jnp.int32, (1, TILES_DEV), 1)
    alive = lane < count_ref[0]
    source = jnp.where(alive, source_ref[...], -1)
    target = jnp.where(alive, target_ref[...], -1)
    from_source = jnp.where(slot == source >> 4, 1.0, 0.0).astype(jnp.bfloat16)
    from_target = jnp.where(slot == target >> 4, 1.0, 0.0).astype(jnp.bfloat16)
    clusters = center_ref.shape[1]
    number = lax.broadcasted_iota(jnp.int32, (clusters, TILES_DEV), 0)
    chosen = jnp.where(number == target, 1.0, 0.0).astype(jnp.bfloat16)
    places = jnp.concatenate([center_ref[...], width_ref[...], jnp.zeros((4, clusters))], axis=0)
    terms = jnp.concatenate(split_exactly(places), axis=0)
    rows = jnp.dot(terms, chosen, preferred_element_type=jnp.float32)
    row = lax.broadcasted_iota(jnp.int32, (24, TILES_DEV), 0)
    local_source = ((source & 15) + 1).astype(jnp.float32)
    local_target = ((target & 15) + 1).astype(jnp.float32)
    rows = jnp.where(row == 4, local_source, rows)
    spread = functools.partial(
        lax.dot_general,
        dimension_numbers=(((1,), (1,)), ((), ())),
        preferred_element_type=jnp.float32,
    )
    out_ref[:, 0:24] = spread(from_source, rows.astype(jnp.bfloat16)) + spread(
        from_target, jnp.where(row == 5, local_target, 0.0).astype(jnp.bfloat16)
    )


def basis_kernel(coord_ref, basis_ref):
    sublane = lax.broadcasted_iota(jnp.int32, (NODES, PTS), 0)

    @pl.loop(0, CL_DEV)
    def _(cluster):
        where = pl.ds(pl.multiple_of(cluster * PTS, PTS), PTS)
        for axis in range(3):
            basis_ref[8 * axis : 8 * axis + 8, where] = lagrange_rows(
                coord_ref[axis : axis + 1, where], sublane
            )


def upward_kernel(domain_ref, width_ref, coord_ref, strength_ref, const_ref, center_ref, all_width_ref, feature_ref, own_ref, same_ref, rows_ref):
    same_ref[...] = const_ref[...]
    domain = domain_ref[0]
    nearby = pl.ds(pl.multiple_of((domain >> 3) * 128, 128), 128)
    places = jnp.concatenate(
        [center_ref[:, nearby], all_width_ref[:, nearby], jnp.zeros((4, 128))], axis=0
    )
    own_ref[...] = pltpu.roll(places, 128 - (domain & 7) * CL_DEV, 1)
    sublane = lax.broadcasted_iota(jnp.int32, (NODES, PTS), 0)
    lane = lax.broadcasted_iota(jnp.int32, (8, 128), 1)

    def one_cluster(cluster, rows):
        where = pl.ds(pl.multiple_of(cluster * PTS, PTS), PTS)
        basis = [lagrange_rows(coord_ref[axis : axis + 1, where], sublane) for axis in range(3)]
        paired = paired_rows(basis[1], basis[2])
        weighted = jnp.concatenate(
            [strength_ref[c : c + 1, where] * basis[0] for c in range(3)], axis=0
        )
        paired_high, paired_low = split_bf16(paired)
        weighted_high, weighted_low = split_bf16(weighted)
        left = jnp.concatenate([weighted_high, weighted_low], axis=0)
        contract = functools.partial(
            lax.dot_general,
            dimension_numbers=(((1,), (1,)), ((), ())),
            preferred_element_type=jnp.float32,
        )
        twice_high = jnp.concatenate([paired_high, paired_high], axis=0)
        twice_low = jnp.concatenate([paired_low, paired_low], axis=0)
        by_high = contract(left, twice_high)
        by_low = contract(weighted_high, twice_low)
        charge = by_high[:24] + by_high[24:] + by_low
        charge = charge * biot_factor
        charges = []
        for c in range(3):
            block = charge[8 * c : 8 * c + 8]
            moved = jnp.concatenate([block[4:], block[:4]], axis=0)
            charges.append(jnp.where(lane < 64, block, moved))
        width = width_ref[domain * CL_DEV + cluster]
        node_x = const_ref[7] * width
        node_y = const_ref[4] * width
        node_z = const_ref[5] * width
        moments = [
            node_y * charges[2] - node_z * charges[1],
            node_z * charges[0] - node_x * charges[2],
            node_x * charges[1] - node_y * charges[0],
        ]
        order = [charges[0], charges[1], charges[2], charges[0], charges[1]] + moments
        for row, value in enumerate(order):
            for group in range(4):
                rows[row : row + 1, 128 * group : 128 * group + 128] = value[group : group + 1]
        high, low = split_bf16(rows[...])
        feature_ref[cluster] = jnp.concatenate([high, low], axis=0)

    @pl.loop(0, CL_DEV, step=2)
    def _(cluster):
        for extra in range(2):
            one_cluster(cluster + extra, rows_ref.at[extra])


def kernel_blocks(width, target_x, square_yz, group_pair, lane_pair):
    highs, lows = [], []
    for lanes in (2 * lane_pair, 2 * lane_pair + 1):
        high_rows, low_rows = [], []
        for group in (2 * group_pair, 2 * group_pair + 1):
            for half in range(2):
                apart_x = target_x[lanes] - width * node_list[group + 4 * half]
                square_x = apart_x * apart_x
                for b in range(0, NODES, 2):
                    pair = []
                    for square in square_yz[b : b + 2]:
                        inverse = lax.rsqrt(square + square_x)
                        pair.append(inverse * inverse * inverse)
                    high, low = split_bf16(jnp.concatenate(pair, axis=0))
                    high_rows.append(high)
                    low_rows.append(low)
        highs.append(jnp.concatenate(high_rows, axis=0))
        lows.append(jnp.concatenate(low_rows, axis=0))
    return jnp.concatenate(highs, axis=1), jnp.concatenate(lows, axis=1)


def tile_kernel(request_ref, own_ref, feature_ref, const_ref, out_ref, order_ref, number_ref, place_ref, number_vmem, place_vmem, semaphore):
    sublane = lax.broadcasted_iota(jnp.int32, (8, 128), 0)
    request = request_ref[...].T
    request = request[0:8] + request[8:16] + request[16:24]
    number_vmem[...] = request.astype(jnp.int32)
    place_vmem[0:8] = request
    place_vmem[8:16] = own_ref[...]
    copies = [
        pltpu.make_async_copy(number_vmem, number_ref, semaphore.at[0]),
        pltpu.make_async_copy(place_vmem, place_ref, semaphore.at[1]),
    ]
    for copy in copies:
        copy.start()
    for copy in copies:
        copy.wait()

    def collect(step, count):
        for extra in range(8):
            peer = step * 8 + extra
            order_ref[count] = peer
            count += (number_ref[4, peer] > 0).astype(jnp.int32)
        return count

    total = lax.fori_loop(0, DOMAINS // 8, collect, 0)
    last = order_ref[jnp.maximum(total - 1, 0)]
    for extra in range(WIDE - 1):
        order_ref[total + extra] = last
    wide = (total + WIDE - NARROW - 1) // WIDE
    narrow = (jnp.maximum(total - wide * WIDE, 0) + NARROW - 1) // NARROW

    def one_tile(peer):
        local_id = number_ref[4, peer] - 1
        source_width = place_ref[11, local_id]
        target_width = place_ref[3, peer]
        shift = [place_ref[axis, peer] - place_ref[8 + axis, local_id] for axis in range(3)]
        target_x = [const_ref[group] * target_width + shift[0] for group in range(4)]
        target_y = const_ref[4] * target_width + shift[1]
        target_z = const_ref[5] * target_width + shift[2]
        apart_z = target_z - const_ref[6] * source_width
        square_z = apart_z * apart_z + smoothing_sq
        square_yz = []
        for b in range(NODES):
            apart_y = target_y - source_width * node_list[b]
            square_yz.append(square_z + apart_y * apart_y)
        feature = feature_ref[local_id]
        for lane_pair in range(2):
            summed = None
            for group_pair in range(2):
                columns = feature[:, 256 * group_pair : 256 * group_pair + 256]
                for block in kernel_blocks(
                    source_width, target_x, square_yz, group_pair, lane_pair
                ):
                    product = jnp.dot(columns, block, preferred_element_type=jnp.float32)
                    summed = product if summed is None else summed + product
            summed = summed[:8] + summed[8:]
            for side in range(2):
                lanes = 2 * lane_pair + side
                block = summed[:, 128 * side : 128 * side + 128]
                first = jnp.where(
                    sublane == 0, target_y, jnp.where(sublane == 1, target_z, target_x[lanes])
                )
                second = jnp.where(
                    sublane == 0, target_z, jnp.where(sublane == 1, target_x[lanes], target_y)
                )
                velocity = (
                    first * pltpu.roll(block, 6, 0)
                    - second * pltpu.roll(block, 7, 0)
                    - pltpu.roll(block, 3, 0)
                )
                for c in range(3):
                    out_ref[peer * 12 + c * 4 + lanes] = velocity[c : c + 1]

    @pl.loop(0, wide)
    def _(step):
        for extra in range(WIDE):
            one_tile(order_ref[step * WIDE + extra])

    @pl.loop(0, narrow)
    def _(step):
        for extra in range(NARROW):
            one_tile(order_ref[wide * WIDE + extra])


def relay_kernel(source_ref, target_ref, in_ref, out_ref):
    slot = lax.broadcasted_iota(jnp.int32, (DOMAINS, TILES_DEV), 0)
    from_source = jnp.where(slot == source_ref[...], 1.0, 0.0).astype(jnp.bfloat16)
    from_target = jnp.where(slot == target_ref[...], 1.0, 0.0).astype(jnp.bfloat16)
    order = lax.dot_general(
        from_target, from_source, (((1,), (1,)), ((), ())), preferred_element_type=jnp.float32
    ).astype(jnp.bfloat16)
    arrived = jnp.dot(
        from_source, jnp.ones((TILES_DEV, 128), jnp.bfloat16), preferred_element_type=jnp.float32
    )
    alive = arrived > 0.5
    for chunk in range(12):
        rows = pl.ds(chunk, DOMAINS, stride=12)
        moved = None
        for term in split_exactly(jnp.where(alive, in_ref[rows, :], 0.0)):
            product = jnp.dot(order, term, preferred_element_type=jnp.float32)
            moved = product if moved is None else moved + product
        out_ref[rows, :] = moved


def downward_kernel(owner_ref, part_ref, basis_ref, out_ref, proxy_ref, held_ref, semaphore):
    owner = owner_ref[:, 5:6].astype(jnp.int32)
    column = lax.broadcasted_iota(jnp.int32, (DOMAINS, CL_DEV), 1)
    assign = (owner == column + 1).astype(jnp.bfloat16)
    gather = functools.partial(
        lax.dot_general,
        dimension_numbers=(((0,), (0,)), ((), ())),
        preferred_element_type=jnp.float32,
    )
    for chunk in range(12):
        high, low = split_bf16(part_ref[pl.ds(chunk, DOMAINS, stride=12), :])
        proxy_ref[chunk * CL_DEV : (chunk + 1) * CL_DEV] = gather(assign, high) + gather(
            assign, low
        )

    def one_cluster(cluster):
        where = pl.ds(cluster * PTS, PTS)
        rows = proxy_ref[pl.ds(cluster, 12, stride=CL_DEV), :]
        near, far = rows[:, :64], rows[:, 64:]
        left = jnp.concatenate(
            [piece[4 * c : 4 * c + 4] for c in range(3) for piece in (near, far)], axis=0
        )
        left_high, left_low = split_bf16(left)
        paired_high, paired_low = split_bf16(
            paired_rows(basis_ref[8:16, where], basis_ref[16:24, where])
        )
        spread = jnp.dot(
            jnp.concatenate([left_high, left_low, left_high], axis=1),
            jnp.concatenate([paired_high, paired_high, paired_low], axis=0),
            preferred_element_type=jnp.float32,
        )
        basis_x = basis_ref[0:8, where]
        for c in range(3):
            held_ref[c : c + 1, where] = jnp.sum(
                spread[8 * c : 8 * c + 8] * basis_x, axis=0, keepdims=True
            )

    copies = []
    for cluster in range(CL_DEV):
        one_cluster(cluster)
        if cluster % 4 == 3:
            where = pl.ds((cluster - 3) * PTS, 4 * PTS)
            copies.append(
                pltpu.make_async_copy(
                    held_ref.at[:, where], out_ref.at[:, where], semaphore.at[cluster // 4]
                )
            )
            copies[-1].start()
    for copy in copies:
        copy.wait()


def in_vmem():
    return pl.BlockSpec(memory_space=pltpu.VMEM)


def in_smem():
    return pl.BlockSpec(memory_space=pltpu.SMEM)


def exchange(value):
    return lax.all_to_all(value, AXES, split_axis=0, concat_axis=0, tiled=True)


def settings(mebibytes):
    return pltpu.CompilerParams(vmem_limit_bytes=mebibytes << 20)


def local(point_coords, strengths, centers, half_widths, tile_source, tile_target, tile_count):
    domain = lax.axis_index(AXES).reshape(1)
    const = jnp.asarray(CONSTANTS)
    message = pl.pallas_call(
        message_kernel,
        out_shape=jax.ShapeDtypeStruct((DOMAINS, 128), jnp.float32),
        in_specs=[in_smem()] + [in_vmem()] * 4,
        out_specs=in_vmem(),
        name="message",
    )(tile_count, tile_source, tile_target, centers, half_widths[None, :])
    received = exchange(message.reshape(DOMAINS, 1, 128)).reshape(DOMAINS, 128)

    features, own_places, kept_const = pl.pallas_call(
        upward_kernel,
        out_shape=(
            jax.ShapeDtypeStruct((CL_DEV, 16, 512), jnp.bfloat16),
            jax.ShapeDtypeStruct((8, 128), jnp.float32),
            jax.ShapeDtypeStruct(const.shape, jnp.float32),
        ),
        in_specs=[in_smem(), in_smem()] + [in_vmem()] * 5,
        out_specs=(in_vmem(), in_vmem(), in_vmem()),
        scratch_shapes=[pltpu.VMEM((2, 8, 512), jnp.float32)],
        compiler_params=settings(8),
        cost_estimate=pl.CostEstimate(flops=10**8, bytes_accessed=10**6, transcendentals=0),
        name="upward",
    )(domain, half_widths, point_coords, strengths, const, centers, half_widths[None, :])

    parts = pl.pallas_call(
        tile_kernel,
        out_shape=jax.ShapeDtypeStruct((DOMAINS * 12, 1, 128), jnp.float32),
        in_specs=[in_vmem()] * 4,
        out_specs=in_vmem(),
        scratch_shapes=[
            pltpu.SMEM((DOMAINS + WIDE,), jnp.int32),
            pltpu.SMEM((8, 128), jnp.int32),
            pltpu.SMEM((16, 128), jnp.float32),
            pltpu.VMEM((8, 128), jnp.int32),
            pltpu.VMEM((16, 128), jnp.float32),
            pltpu.SemaphoreType.DMA((2,)),
        ],
        compiler_params=settings(8),
        name="tiles",
    )(received, own_places, features, kept_const)

    relayed = exchange(parts.reshape(DOMAINS, 1, 1536))
    alive = (jnp.arange(TILES_DEV) < tile_count[0])[None, :]
    source_owners = jnp.where(alive, tile_source >> 4, -1)
    target_owners = jnp.where(alive, tile_target >> 4, -1)
    ordered = pl.pallas_call(
        relay_kernel,
        out_shape=jax.ShapeDtypeStruct((DOMAINS * 12, 128), jnp.float32),
        in_specs=[in_vmem()] * 3,
        out_specs=in_vmem(),
        compiler_params=settings(4),
        name="relay",
    )(source_owners, target_owners, relayed.reshape(DOMAINS * 12, 128))
    arrived = exchange(ordered.reshape(DOMAINS, 1, 1536))

    basis = pl.pallas_call(
        basis_kernel,
        out_shape=jax.ShapeDtypeStruct((24, CL_DEV * PTS), jnp.float32),
        in_specs=[in_vmem()],
        out_specs=in_vmem(),
        compiler_params=settings(8),
        cost_estimate=pl.CostEstimate(flops=10**8, bytes_accessed=2 * 10**6, transcendentals=0),
        name="basis",
    )(point_coords)
    return pl.pallas_call(
        downward_kernel,
        out_shape=jax.ShapeDtypeStruct((3, CL_DEV * PTS), jnp.float32),
        in_specs=[in_vmem(), in_vmem(), in_vmem()],
        out_specs=pl.BlockSpec(memory_space=pl.ANY),
        scratch_shapes=[
            pltpu.VMEM((12 * CL_DEV, 128), jnp.float32),
            pltpu.VMEM((3, CL_DEV * PTS), jnp.float32),
            pltpu.SemaphoreType.DMA((CL_DEV // 4,)),
        ],
        compiler_params=settings(8),
        name="downward",
    )(received, arrived.reshape(DOMAINS * 12, 128), basis)


def solution(mesh):
    return jax.shard_map(
        local,
        mesh=mesh,
        in_specs=(
            P(None, AXES),
            P(None, AXES),
            P(),
            P(),
            P(AXES, None),
            P(AXES, None),
            P(AXES),
        ),
        out_specs=P(None, AXES),
        check_vma=False,
    )
```

```python
import functools
import math

import jax
import jax.numpy as jnp
import numpy as np
from jax import lax
from jax.experimental import pallas as pl
from jax.experimental.pallas import tpu as pltpu
from jax.sharding import PartitionSpec as P

CL_DEV = 16
PTS = 1024
DEG = 7
TILES_DEV = 128
DOMAINS = 128
NODES = DEG + 1
WIDE = 8
NARROW = 4
AXES = ("gx", "gy")

smoothing_sq = 0.01
biot_factor = -0.07957747154594767

node_values = np.cos(np.pi * np.arange(NODES) / DEG)
node_list = [float(v) for v in node_values.astype(np.float32)]
node_scales = [
    1.0 / math.prod(node_list[a] - node_list[m] for m in range(NODES) if m != a)
    for a in range(NODES)
]


def build_constants():
    nodes = node_values.astype(np.float32)
    lane = np.arange(128)
    table = np.zeros((8, 8, 128), np.float32)
    for group in range(4):
        table[group] = nodes[group + 4 * (lane // 64)][None, :]
    table[4] = nodes[(lane // 8) % 8][None, :]
    table[5] = nodes[lane % 8][None, :]
    table[6] = nodes[:, None]
    table[7, :4] = table[:4, 0]
    return table


CONSTANTS = build_constants()


def split_bf16(value):
    high = value.astype(jnp.bfloat16)
    return high, (value - high.astype(jnp.float32)).astype(jnp.bfloat16)


def lagrange_rows(row, sublane):
    spread = jnp.broadcast_to(row, (NODES, row.shape[1]))
    result = None
    for m in range(NODES):
        factor = jnp.where(sublane == m, node_scales[m], spread - node_list[m])
        result = factor if result is None else result * factor
    return result


def paired_rows(basis_y, basis_z):
    return jnp.concatenate([basis_y[b : b + 1] * basis_z for b in range(NODES)], axis=0)


def split_exactly(value):
    high = value.astype(jnp.bfloat16)
    rest = value - high.astype(jnp.float32)
    middle = rest.astype(jnp.bfloat16)
    return high, middle, (rest - middle.astype(jnp.float32)).astype(jnp.bfloat16)


def message_kernel(count_ref, source_ref, target_ref, center_ref, width_ref, out_ref, owner_ref):
    slot = lax.broadcasted_iota(jnp.int32, (DOMAINS, TILES_DEV), 0)
    lane = lax.broadcasted_iota(jnp.int32, (1, TILES_DEV), 1)
    alive = lane < count_ref[0]
    source = jnp.where(alive, source_ref[...], -1)
    target = jnp.where(alive, target_ref[...], -1)
    owner_ref[0:1] = source >> 4
    owner_ref[1:2] = target >> 4
    from_source = jnp.where(slot == source >> 4, 1.0, 0.0).astype(jnp.bfloat16)
    from_target = jnp.where(slot == target >> 4, 1.0, 0.0).astype(jnp.bfloat16)
    clusters = center_ref.shape[1]
    number = lax.broadcasted_iota(jnp.int32, (clusters, TILES_DEV), 0)
    chosen = jnp.where(number == target, 1.0, 0.0).astype(jnp.bfloat16)
    places = jnp.concatenate([center_ref[...], width_ref[...], jnp.zeros((4, clusters))], axis=0)
    terms = jnp.concatenate(split_exactly(places), axis=0)
    rows = jnp.dot(terms, chosen, preferred_element_type=jnp.float32)
    row = lax.broadcasted_iota(jnp.int32, (24, TILES_DEV), 0)
    local_source = ((source & 15) + 1).astype(jnp.float32)
    local_target = ((target & 15) + 1).astype(jnp.float32)
    rows = jnp.where(row == 4, local_source, rows)
    spread = functools.partial(
        lax.dot_general,
        dimension_numbers=(((1,), (1,)), ((), ())),
        preferred_element_type=jnp.float32,
    )
    out_ref[:, 0:24] = spread(from_source, rows.astype(jnp.bfloat16)) + spread(
        from_target, jnp.where(row == 5, local_target, 0.0).astype(jnp.bfloat16)
    )


def upward_kernel(domain_ref, width_ref, coord_ref, strength_ref, const_ref, center_ref, all_width_ref, feature_ref, own_ref, same_ref, basis_ref, rows_ref):
    same_ref[...] = const_ref[...]
    domain = domain_ref[0]
    nearby = pl.ds(pl.multiple_of((domain >> 3) * 128, 128), 128)
    places = jnp.concatenate(
        [center_ref[:, nearby], all_width_ref[:, nearby], jnp.zeros((4, 128))], axis=0
    )
    own_ref[...] = pltpu.roll(places, 128 - (domain & 7) * CL_DEV, 1)
    sublane = lax.broadcasted_iota(jnp.int32, (NODES, PTS), 0)
    lane = lax.broadcasted_iota(jnp.int32, (8, 128), 1)

    def one_cluster(cluster, rows):
        where = pl.ds(pl.multiple_of(cluster * PTS, PTS), PTS)
        basis = [lagrange_rows(coord_ref[axis : axis + 1, where], sublane) for axis in range(3)]
        for axis in range(3):
            basis_ref[8 * axis : 8 * axis + 8, where] = basis[axis]
        paired = paired_rows(basis[1], basis[2])
        weighted = jnp.concatenate(
            [strength_ref[c : c + 1, where] * basis[0] for c in range(3)], axis=0
        )
        paired_high, paired_low = split_bf16(paired)
        weighted_high, weighted_low = split_bf16(weighted)
        left = jnp.concatenate([weighted_high, weighted_low], axis=0)
        contract = functools.partial(
            lax.dot_general,
            dimension_numbers=(((1,), (1,)), ((), ())),
            preferred_element_type=jnp.float32,
        )
        twice_high = jnp.concatenate([paired_high, paired_high], axis=0)
        twice_low = jnp.concatenate([paired_low, paired_low], axis=0)
        by_high = contract(left, twice_high)
        by_low = contract(weighted_high, twice_low)
        charge = by_high[:24] + by_high[24:] + by_low
        charge = charge * biot_factor
        charges = []
        for c in range(3):
            block = charge[8 * c : 8 * c + 8]
            moved = jnp.concatenate([block[4:], block[:4]], axis=0)
            charges.append(jnp.where(lane < 64, block, moved))
        width = width_ref[domain * CL_DEV + cluster]
        node_x = const_ref[7] * width
        node_y = const_ref[4] * width
        node_z = const_ref[5] * width
        moments = [
            node_y * charges[2] - node_z * charges[1],
            node_z * charges[0] - node_x * charges[2],
            node_x * charges[1] - node_y * charges[0],
        ]
        order = [charges[0], charges[1], charges[2], charges[0], charges[1]] + moments
        for row, value in enumerate(order):
            for group in range(4):
                rows[row : row + 1, 128 * group : 128 * group + 128] = value[group : group + 1]
        high, low = split_bf16(rows[...])
        feature_ref[cluster] = jnp.concatenate([high, low], axis=0)

    @pl.loop(0, CL_DEV, step=2)
    def _(cluster):
        for extra in range(2):
            one_cluster(cluster + extra, rows_ref.at[extra])


def kernel_blocks(width, target_x, square_yz, group_pair, lane_pair):
    highs, lows = [], []
    for lanes in (2 * lane_pair, 2 * lane_pair + 1):
        high_rows, low_rows = [], []
        for group in (2 * group_pair, 2 * group_pair + 1):
            for half in range(2):
                apart_x = target_x[lanes] - width * node_list[group + 4 * half]
                square_x = apart_x * apart_x
                for b in range(0, NODES, 2):
                    pair = []
                    for square in square_yz[b : b + 2]:
                        inverse = lax.rsqrt(square + square_x)
                        pair.append(inverse * inverse * inverse)
                    high, low = split_bf16(jnp.concatenate(pair, axis=0))
                    high_rows.append(high)
                    low_rows.append(low)
        highs.append(jnp.concatenate(high_rows, axis=0))
        lows.append(jnp.concatenate(low_rows, axis=0))
    return jnp.concatenate(highs, axis=1), jnp.concatenate(lows, axis=1)


def tile_kernel(request_ref, own_ref, feature_ref, const_ref, out_ref, order_ref, number_ref, place_ref, number_vmem, place_vmem, semaphore):
    sublane = lax.broadcasted_iota(jnp.int32, (8, 128), 0)
    request = request_ref[...].T
    request = request[0:8] + request[8:16] + request[16:24]
    number_vmem[...] = request.astype(jnp.int32)
    place_vmem[0:8] = request
    place_vmem[8:16] = own_ref[...]
    copies = [
        pltpu.make_async_copy(number_vmem, number_ref, semaphore.at[0]),
        pltpu.make_async_copy(place_vmem, place_ref, semaphore.at[1]),
    ]
    for copy in copies:
        copy.start()
    for copy in copies:
        copy.wait()

    def collect(step, count):
        for extra in range(8):
            peer = step * 8 + extra
            order_ref[count] = peer
            count += (number_ref[4, peer] > 0).astype(jnp.int32)
        return count

    total = lax.fori_loop(0, DOMAINS // 8, collect, 0)
    last = order_ref[jnp.maximum(total - 1, 0)]
    for extra in range(WIDE - 1):
        order_ref[total + extra] = last
    wide = (total + WIDE - NARROW - 1) // WIDE
    narrow = (jnp.maximum(total - wide * WIDE, 0) + NARROW - 1) // NARROW

    def one_tile(peer):
        local_id = number_ref[4, peer] - 1
        source_width = place_ref[11, local_id]
        target_width = place_ref[3, peer]
        shift = [place_ref[axis, peer] - place_ref[8 + axis, local_id] for axis in range(3)]
        target_x = [const_ref[group] * target_width + shift[0] for group in range(4)]
        target_y = const_ref[4] * target_width + shift[1]
        target_z = const_ref[5] * target_width + shift[2]
        apart_z = target_z - const_ref[6] * source_width
        square_z = apart_z * apart_z + smoothing_sq
        square_yz = []
        for b in range(NODES):
            apart_y = target_y - source_width * node_list[b]
            square_yz.append(square_z + apart_y * apart_y)
        feature = feature_ref[local_id]
        for lane_pair in range(2):
            summed = None
            for group_pair in range(2):
                columns = feature[:, 256 * group_pair : 256 * group_pair + 256]
                for block in kernel_blocks(
                    source_width, target_x, square_yz, group_pair, lane_pair
                ):
                    product = jnp.dot(columns, block, preferred_element_type=jnp.float32)
                    summed = product if summed is None else summed + product
            summed = summed[:8] + summed[8:]
            for side in range(2):
                lanes = 2 * lane_pair + side
                block = summed[:, 128 * side : 128 * side + 128]
                first = jnp.where(
                    sublane == 0, target_y, jnp.where(sublane == 1, target_z, target_x[lanes])
                )
                second = jnp.where(
                    sublane == 0, target_z, jnp.where(sublane == 1, target_x[lanes], target_y)
                )
                velocity = (
                    first * pltpu.roll(block, 6, 0)
                    - second * pltpu.roll(block, 7, 0)
                    - pltpu.roll(block, 3, 0)
                )
                for c in range(3):
                    out_ref[peer * 12 + c * 4 + lanes] = velocity[c : c + 1]

    @pl.loop(0, wide)
    def _(step):
        for extra in range(WIDE):
            one_tile(order_ref[step * WIDE + extra])

    @pl.loop(0, narrow)
    def _(step):
        for extra in range(NARROW):
            one_tile(order_ref[wide * WIDE + extra])


def relay_kernel(owner_ref, in_ref, out_ref):
    slot = lax.broadcasted_iota(jnp.int32, (DOMAINS, TILES_DEV), 0)
    from_source = jnp.where(slot == owner_ref[0:1], 1.0, 0.0).astype(jnp.bfloat16)
    from_target = jnp.where(slot == owner_ref[1:2], 1.0, 0.0).astype(jnp.bfloat16)
    order = lax.dot_general(
        from_target, from_source, (((1,), (1,)), ((), ())), preferred_element_type=jnp.float32
    ).astype(jnp.bfloat16)
    arrived = jnp.dot(
        from_source, jnp.ones((TILES_DEV, 128), jnp.bfloat16), preferred_element_type=jnp.float32
    )
    alive = arrived > 0.5
    for chunk in range(12):
        rows = pl.ds(chunk, DOMAINS, stride=12)
        moved = None
        for term in split_exactly(jnp.where(alive, in_ref[rows, :], 0.0)):
            product = jnp.dot(order, term, preferred_element_type=jnp.float32)
            moved = product if moved is None else moved + product
        out_ref[rows, :] = moved


def downward_kernel(owner_ref, part_ref, basis_ref, out_ref, proxy_ref, held_ref, semaphore):
    owner = owner_ref[:, 5:6].astype(jnp.int32)
    column = lax.broadcasted_iota(jnp.int32, (DOMAINS, CL_DEV), 1)
    assign = (owner == column + 1).astype(jnp.bfloat16)
    gather = functools.partial(
        lax.dot_general,
        dimension_numbers=(((0,), (0,)), ((), ())),
        preferred_element_type=jnp.float32,
    )
    for chunk in range(12):
        high, low = split_bf16(part_ref[pl.ds(chunk, DOMAINS, stride=12), :])
        proxy_ref[chunk * CL_DEV : (chunk + 1) * CL_DEV] = gather(assign, high) + gather(
            assign, low
        )

    def one_cluster(cluster):
        where = pl.ds(cluster * PTS, PTS)
        rows = proxy_ref[pl.ds(cluster, 12, stride=CL_DEV), :]
        near, far = rows[:, :64], rows[:, 64:]
        left = jnp.concatenate(
            [piece[4 * c : 4 * c + 4] for c in range(3) for piece in (near, far)], axis=0
        )
        left_high, left_low = split_bf16(left)
        paired_high, paired_low = split_bf16(
            paired_rows(basis_ref[8:16, where], basis_ref[16:24, where])
        )
        spread = jnp.dot(
            jnp.concatenate([left_high, left_low, left_high], axis=1),
            jnp.concatenate([paired_high, paired_high, paired_low], axis=0),
            preferred_element_type=jnp.float32,
        )
        basis_x = basis_ref[0:8, where]
        for c in range(3):
            held_ref[c : c + 1, where] = jnp.sum(
                spread[8 * c : 8 * c + 8] * basis_x, axis=0, keepdims=True
            )

    copies = []
    for cluster in range(CL_DEV):
        one_cluster(cluster)
        if cluster % 4 == 3:
            where = pl.ds((cluster - 3) * PTS, 4 * PTS)
            copies.append(
                pltpu.make_async_copy(
                    held_ref.at[:, where], out_ref.at[:, where], semaphore.at[cluster // 4]
                )
            )
            copies[-1].start()
    for copy in copies:
        copy.wait()


def in_vmem():
    return pl.BlockSpec(memory_space=pltpu.VMEM)


def in_smem():
    return pl.BlockSpec(memory_space=pltpu.SMEM)


def exchange(value):
    return lax.all_to_all(value, AXES, split_axis=0, concat_axis=0, tiled=True)


def settings(mebibytes):
    return pltpu.CompilerParams(vmem_limit_bytes=mebibytes << 20)


def local(point_coords, strengths, centers, half_widths, tile_source, tile_target, tile_count):
    domain = lax.axis_index(AXES).reshape(1)
    const = jnp.asarray(CONSTANTS)
    message, owners = pl.pallas_call(
        message_kernel,
        out_shape=(
            jax.ShapeDtypeStruct((DOMAINS, 128), jnp.float32),
            jax.ShapeDtypeStruct((2, TILES_DEV), jnp.int32),
        ),
        in_specs=[in_smem()] + [in_vmem()] * 4,
        out_specs=(in_vmem(), in_vmem()),
        name="message",
    )(tile_count, tile_source, tile_target, centers, half_widths[None, :])
    received = exchange(message.reshape(DOMAINS, 1, 128)).reshape(DOMAINS, 128)

    features, own_places, kept_const, basis = pl.pallas_call(
        upward_kernel,
        out_shape=(
            jax.ShapeDtypeStruct((CL_DEV, 16, 512), jnp.bfloat16),
            jax.ShapeDtypeStruct((8, 128), jnp.float32),
            jax.ShapeDtypeStruct(const.shape, jnp.float32),
            jax.ShapeDtypeStruct((24, CL_DEV * PTS), jnp.float32),
        ),
        in_specs=[in_smem(), in_smem()] + [in_vmem()] * 5,
        out_specs=(in_vmem(),) * 4,
        scratch_shapes=[pltpu.VMEM((2, 8, 512), jnp.float32)],
        compiler_params=settings(8),
        cost_estimate=pl.CostEstimate(flops=10**8, bytes_accessed=10**6, transcendentals=0),
        name="upward",
    )(domain, half_widths, point_coords, strengths, const, centers, half_widths[None, :])

    parts = pl.pallas_call(
        tile_kernel,
        out_shape=jax.ShapeDtypeStruct((DOMAINS * 12, 1, 128), jnp.float32),
        in_specs=[in_vmem()] * 4,
        out_specs=in_vmem(),
        scratch_shapes=[
            pltpu.SMEM((DOMAINS + WIDE,), jnp.int32),
            pltpu.SMEM((8, 128), jnp.int32),
            pltpu.SMEM((16, 128), jnp.float32),
            pltpu.VMEM((8, 128), jnp.int32),
            pltpu.VMEM((16, 128), jnp.float32),
            pltpu.SemaphoreType.DMA((2,)),
        ],
        compiler_params=settings(8),
        name="tiles",
    )(received, own_places, features, kept_const)

    relayed = exchange(parts.reshape(DOMAINS, 1, 1536))
    ordered = pl.pallas_call(
        relay_kernel,
        out_shape=jax.ShapeDtypeStruct((DOMAINS * 12, 128), jnp.float32),
        in_specs=[in_vmem()] * 2,
        out_specs=in_vmem(),
        compiler_params=settings(4),
        name="relay",
    )(owners, relayed.reshape(DOMAINS * 12, 128))
    arrived = exchange(ordered.reshape(DOMAINS, 1, 1536))

    return pl.pallas_call(
        downward_kernel,
        out_shape=jax.ShapeDtypeStruct((3, CL_DEV * PTS), jnp.float32),
        in_specs=[in_vmem(), in_vmem(), in_vmem()],
        out_specs=pl.BlockSpec(memory_space=pl.ANY),
        scratch_shapes=[
            pltpu.VMEM((12 * CL_DEV, 128), jnp.float32),
            pltpu.VMEM((3, CL_DEV * PTS), jnp.float32),
            pltpu.SemaphoreType.DMA((CL_DEV // 4,)),
        ],
        compiler_params=settings(8),
        name="downward",
    )(received, arrived.reshape(DOMAINS * 12, 128), basis)


def solution(mesh):
    return jax.shard_map(
        local,
        mesh=mesh,
        in_specs=(
            P(None, AXES),
            P(None, AXES),
            P(),
            P(),
            P(AXES, None),
            P(AXES, None),
            P(AXES),
        ),
        out_specs=P(None, AXES),
        check_vma=False,
    )
```

```python
import functools
import math

import jax
import jax.numpy as jnp
import numpy as np
from jax import lax
from jax.experimental import pallas as pl
from jax.experimental.pallas import tpu as pltpu
from jax.sharding import PartitionSpec as P

CL_DEV = 16
PTS = 1024
DEG = 7
TILES_DEV = 128
DOMAINS = 128
NODES = DEG + 1
GROUPS = (8, 4, 2, 1)
AXES = ("gx", "gy")

smoothing_sq = 0.01
biot_factor = -0.07957747154594767

node_values = np.cos(np.pi * np.arange(NODES) / DEG)
node_list = [float(v) for v in node_values.astype(np.float32)]
node_scales = [
    1.0 / math.prod(node_list[a] - node_list[m] for m in range(NODES) if m != a)
    for a in range(NODES)
]


def build_constants():
    nodes = node_values.astype(np.float32)
    lane = np.arange(128)
    table = np.zeros((8, 8, 128), np.float32)
    for group in range(4):
        table[group] = nodes[group + 4 * (lane // 64)][None, :]
    table[4] = nodes[(lane // 8) % 8][None, :]
    table[5] = nodes[lane % 8][None, :]
    table[6] = nodes[:, None]
    table[7, :4] = table[:4, 0]
    return table


CONSTANTS = build_constants()


def split_bf16(value):
    high = value.astype(jnp.bfloat16)
    return high, (value - high.astype(jnp.float32)).astype(jnp.bfloat16)


def lagrange_rows(row, sublane):
    spread = jnp.broadcast_to(row, (NODES, row.shape[1]))
    result = None
    for m in range(NODES):
        factor = jnp.where(sublane == m, node_scales[m], spread - node_list[m])
        result = factor if result is None else result * factor
    return result


def paired_rows(basis_y, basis_z):
    return jnp.concatenate([basis_y[b : b + 1] * basis_z for b in range(NODES)], axis=0)


def split_exactly(value):
    high = value.astype(jnp.bfloat16)
    rest = value - high.astype(jnp.float32)
    middle = rest.astype(jnp.bfloat16)
    return high, middle, (rest - middle.astype(jnp.float32)).astype(jnp.bfloat16)


def message_kernel(count_ref, source_ref, target_ref, center_ref, width_ref, out_ref, owner_ref):
    slot = lax.broadcasted_iota(jnp.int32, (DOMAINS, TILES_DEV), 0)
    lane = lax.broadcasted_iota(jnp.int32, (1, TILES_DEV), 1)
    alive = lane < count_ref[0]
    source = jnp.where(alive, source_ref[...], -1)
    target = jnp.where(alive, target_ref[...], -1)
    owner_ref[0:1] = source >> 4
    owner_ref[1:2] = target >> 4
    from_source = jnp.where(slot == source >> 4, 1.0, 0.0).astype(jnp.bfloat16)
    from_target = jnp.where(slot == target >> 4, 1.0, 0.0).astype(jnp.bfloat16)
    clusters = center_ref.shape[1]
    number = lax.broadcasted_iota(jnp.int32, (clusters, TILES_DEV), 0)
    chosen = jnp.where(number == target, 1.0, 0.0).astype(jnp.bfloat16)
    places = jnp.concatenate([center_ref[...], width_ref[...], jnp.zeros((4, clusters))], axis=0)
    terms = jnp.concatenate(split_exactly(places), axis=0)
    rows = jnp.dot(terms, chosen, preferred_element_type=jnp.float32)
    row = lax.broadcasted_iota(jnp.int32, (24, TILES_DEV), 0)
    local_source = ((source & 15) + 1).astype(jnp.float32)
    local_target = ((target & 15) + 1).astype(jnp.float32)
    rows = jnp.where(row == 4, local_source, rows)
    spread = functools.partial(
        lax.dot_general,
        dimension_numbers=(((1,), (1,)), ((), ())),
        preferred_element_type=jnp.float32,
    )
    out_ref[:, 0:24] = spread(from_source, rows.astype(jnp.bfloat16)) + spread(
        from_target, jnp.where(row == 5, local_target, 0.0).astype(jnp.bfloat16)
    )


def upward_kernel(domain_ref, width_ref, coord_ref, strength_ref, const_ref, center_ref, all_width_ref, feature_ref, own_ref, same_ref, basis_ref, rows_ref):
    same_ref[...] = const_ref[...]
    domain = domain_ref[0]
    nearby = pl.ds(pl.multiple_of((domain >> 3) * 128, 128), 128)
    places = jnp.concatenate(
        [center_ref[:, nearby], all_width_ref[:, nearby], jnp.zeros((4, 128))], axis=0
    )
    own_ref[...] = pltpu.roll(places, 128 - (domain & 7) * CL_DEV, 1)
    sublane = lax.broadcasted_iota(jnp.int32, (NODES, PTS), 0)
    lane = lax.broadcasted_iota(jnp.int32, (8, 128), 1)

    def one_cluster(cluster, rows):
        where = pl.ds(pl.multiple_of(cluster * PTS, PTS), PTS)
        basis = [lagrange_rows(coord_ref[axis : axis + 1, where], sublane) for axis in range(3)]
        for axis in range(3):
            basis_ref[8 * axis : 8 * axis + 8, where] = basis[axis]
        paired = paired_rows(basis[1], basis[2])
        weighted = jnp.concatenate(
            [strength_ref[c : c + 1, where] * basis[0] for c in range(3)], axis=0
        )
        paired_high, paired_low = split_bf16(paired)
        weighted_high, weighted_low = split_bf16(weighted)
        left = jnp.concatenate([weighted_high, weighted_low], axis=0)
        contract = functools.partial(
            lax.dot_general,
            dimension_numbers=(((1,), (1,)), ((), ())),
            preferred_element_type=jnp.float32,
        )
        twice_high = jnp.concatenate([paired_high, paired_high], axis=0)
        twice_low = jnp.concatenate([paired_low, paired_low], axis=0)
        by_high = contract(left, twice_high)
        by_low = contract(weighted_high, twice_low)
        charge = by_high[:24] + by_high[24:] + by_low
        charge = charge * biot_factor
        charges = []
        for c in range(3):
            block = charge[8 * c : 8 * c + 8]
            moved = jnp.concatenate([block[4:], block[:4]], axis=0)
            charges.append(jnp.where(lane < 64, block, moved))
        width = width_ref[domain * CL_DEV + cluster]
        node_x = const_ref[7] * width
        node_y = const_ref[4] * width
        node_z = const_ref[5] * width
        moments = [
            node_y * charges[2] - node_z * charges[1],
            node_z * charges[0] - node_x * charges[2],
            node_x * charges[1] - node_y * charges[0],
        ]
        order = [charges[0], charges[1], charges[2], charges[0], charges[1]] + moments
        for row, value in enumerate(order):
            for group in range(4):
                rows[row : row + 1, 128 * group : 128 * group + 128] = value[group : group + 1]
        high, low = split_bf16(rows[...])
        feature_ref[cluster] = jnp.concatenate([high, low], axis=0)

    @pl.loop(0, CL_DEV, step=2)
    def _(cluster):
        for extra in range(2):
            one_cluster(cluster + extra, rows_ref.at[extra])


def kernel_blocks(width, target_x, square_yz, group_pair, lane_pair):
    highs, lows = [], []
    for lanes in (2 * lane_pair, 2 * lane_pair + 1):
        high_rows, low_rows = [], []
        for group in (2 * group_pair, 2 * group_pair + 1):
            for half in range(2):
                apart_x = target_x[lanes] - width * node_list[group + 4 * half]
                square_x = apart_x * apart_x
                for b in range(0, NODES, 2):
                    pair = []
                    for square in square_yz[b : b + 2]:
                        inverse = lax.rsqrt(square + square_x)
                        pair.append(inverse * inverse * inverse)
                    high, low = split_bf16(jnp.concatenate(pair, axis=0))
                    high_rows.append(high)
                    low_rows.append(low)
        highs.append(jnp.concatenate(high_rows, axis=0))
        lows.append(jnp.concatenate(low_rows, axis=0))
    return jnp.concatenate(highs, axis=1), jnp.concatenate(lows, axis=1)


def tile_kernel(request_ref, own_ref, feature_ref, const_ref, out_ref, order_ref, number_ref, place_ref, number_vmem, place_vmem, semaphore):
    sublane = lax.broadcasted_iota(jnp.int32, (8, 128), 0)
    request = request_ref[...].T
    request = request[0:8] + request[8:16] + request[16:24]
    number_vmem[...] = request.astype(jnp.int32)
    place_vmem[0:8] = request
    place_vmem[8:16] = own_ref[...]
    copies = [
        pltpu.make_async_copy(number_vmem, number_ref, semaphore.at[0]),
        pltpu.make_async_copy(place_vmem, place_ref, semaphore.at[1]),
    ]
    for copy in copies:
        copy.start()
    for copy in copies:
        copy.wait()

    total = 0
    for peer in range(DOMAINS):
        order_ref[total] = peer
        total += (number_ref[4, peer] > 0).astype(jnp.int32)
    order_ref[total] = order_ref[jnp.maximum(total - 1, 0)]
    padded = total + (total % 4 == 3).astype(jnp.int32)

    def one_tile(peer):
        local_id = number_ref[4, peer] - 1
        source_width = place_ref[11, local_id]
        target_width = place_ref[3, peer]
        shift = [place_ref[axis, peer] - place_ref[8 + axis, local_id] for axis in range(3)]
        target_x = [const_ref[group] * target_width + shift[0] for group in range(4)]
        target_y = const_ref[4] * target_width + shift[1]
        target_z = const_ref[5] * target_width + shift[2]
        apart_z = target_z - const_ref[6] * source_width
        square_z = apart_z * apart_z + smoothing_sq
        square_yz = []
        for b in range(NODES):
            apart_y = target_y - source_width * node_list[b]
            square_yz.append(square_z + apart_y * apart_y)
        feature = feature_ref[local_id]
        first_rows = jnp.where(sublane == 0, target_y, target_z)
        second_rows = jnp.where(sublane == 0, target_z, target_y)
        for lane_pair in range(2):
            summed = None
            for group_pair in range(2):
                columns = feature[:, 256 * group_pair : 256 * group_pair + 256]
                for block in kernel_blocks(
                    source_width, target_x, square_yz, group_pair, lane_pair
                ):
                    product = jnp.dot(columns, block, preferred_element_type=jnp.float32)
                    summed = product if summed is None else summed + product
            summed = summed[:8] + summed[8:]
            for side in range(2):
                lanes = 2 * lane_pair + side
                block = summed[:, 128 * side : 128 * side + 128]
                first = jnp.where(sublane < 2, first_rows, target_x[lanes])
                second = jnp.where(sublane == 1, target_x[lanes], second_rows)
                velocity = (
                    first * pltpu.roll(block, 6, 0)
                    - second * pltpu.roll(block, 7, 0)
                    - pltpu.roll(block, 3, 0)
                )
                for c in range(3):
                    out_ref[peer * 12 + c * 4 + lanes] = velocity[c : c + 1]

    done = 0
    for size in GROUPS:
        rounds = (padded - done) // size

        @pl.loop(0, rounds)
        def _(step):
            for extra in range(size):
                one_tile(order_ref[done + step * size + extra])

        done += rounds * size


def relay_kernel(owner_ref, in_ref, out_ref):
    slot = lax.broadcasted_iota(jnp.int32, (DOMAINS, TILES_DEV), 0)
    from_source = jnp.where(slot == owner_ref[0:1], 1.0, 0.0).astype(jnp.bfloat16)
    from_target = jnp.where(slot == owner_ref[1:2], 1.0, 0.0).astype(jnp.bfloat16)
    order = lax.dot_general(
        from_target, from_source, (((1,), (1,)), ((), ())), preferred_element_type=jnp.float32
    ).astype(jnp.bfloat16)
    arrived = jnp.dot(
        from_source, jnp.ones((TILES_DEV, 128), jnp.bfloat16), preferred_element_type=jnp.float32
    )
    alive = arrived > 0.5
    for chunk in range(12):
        rows = pl.ds(chunk, DOMAINS, stride=12)
        moved = None
        for term in split_exactly(jnp.where(alive, in_ref[rows, :], 0.0)):
            product = jnp.dot(order, term, preferred_element_type=jnp.float32)
            moved = product if moved is None else moved + product
        out_ref[rows, :] = moved


def downward_kernel(owner_ref, part_ref, basis_ref, out_ref, proxy_ref, held_ref, semaphore):
    owner = owner_ref[:, 5:6].astype(jnp.int32)
    column = lax.broadcasted_iota(jnp.int32, (DOMAINS, CL_DEV), 1)
    assign = (owner == column + 1).astype(jnp.bfloat16)
    gather = functools.partial(
        lax.dot_general,
        dimension_numbers=(((0,), (0,)), ((), ())),
        preferred_element_type=jnp.float32,
    )
    for chunk in range(12):
        high, low = split_bf16(part_ref[pl.ds(chunk, DOMAINS, stride=12), :])
        proxy_ref[chunk * CL_DEV : (chunk + 1) * CL_DEV] = gather(assign, high) + gather(
            assign, low
        )

    def one_cluster(cluster):
        where = pl.ds(cluster * PTS, PTS)
        rows = proxy_ref[pl.ds(cluster, 12, stride=CL_DEV), :]
        near, far = rows[:, :64], rows[:, 64:]
        left = jnp.concatenate(
            [piece[4 * c : 4 * c + 4] for c in range(3) for piece in (near, far)], axis=0
        )
        left_high, left_low = split_bf16(left)
        paired_high, paired_low = split_bf16(
            paired_rows(basis_ref[8:16, where], basis_ref[16:24, where])
        )
        spread = jnp.dot(
            jnp.concatenate([left_high, left_low, left_high], axis=1),
            jnp.concatenate([paired_high, paired_high, paired_low], axis=0),
            preferred_element_type=jnp.float32,
        )
        basis_x = basis_ref[0:8, where]
        for c in range(3):
            held_ref[c : c + 1, where] = jnp.sum(
                spread[8 * c : 8 * c + 8] * basis_x, axis=0, keepdims=True
            )

    copies = []
    for cluster in range(CL_DEV):
        one_cluster(cluster)
        if cluster % 4 == 3:
            where = pl.ds((cluster - 3) * PTS, 4 * PTS)
            copies.append(
                pltpu.make_async_copy(
                    held_ref.at[:, where], out_ref.at[:, where], semaphore.at[cluster // 4]
                )
            )
            copies[-1].start()
    for copy in copies:
        copy.wait()


def in_vmem():
    return pl.BlockSpec(memory_space=pltpu.VMEM)


def in_smem():
    return pl.BlockSpec(memory_space=pltpu.SMEM)


def exchange(value):
    return lax.all_to_all(value, AXES, split_axis=0, concat_axis=0, tiled=True)


def settings(mebibytes):
    return pltpu.CompilerParams(vmem_limit_bytes=mebibytes << 20)


def local(point_coords, strengths, centers, half_widths, tile_source, tile_target, tile_count):
    domain = lax.axis_index(AXES).reshape(1)
    const = jnp.asarray(CONSTANTS)
    message, owners = pl.pallas_call(
        message_kernel,
        out_shape=(
            jax.ShapeDtypeStruct((DOMAINS, 128), jnp.float32),
            jax.ShapeDtypeStruct((2, TILES_DEV), jnp.int32),
        ),
        in_specs=[in_smem()] + [in_vmem()] * 4,
        out_specs=(in_vmem(), in_vmem()),
        name="message",
    )(tile_count, tile_source, tile_target, centers, half_widths[None, :])
    received = exchange(message.reshape(DOMAINS, 1, 128)).reshape(DOMAINS, 128)

    features, own_places, kept_const, basis = pl.pallas_call(
        upward_kernel,
        out_shape=(
            jax.ShapeDtypeStruct((CL_DEV, 16, 512), jnp.bfloat16),
            jax.ShapeDtypeStruct((8, 128), jnp.float32),
            jax.ShapeDtypeStruct(const.shape, jnp.float32),
            jax.ShapeDtypeStruct((24, CL_DEV * PTS), jnp.float32),
        ),
        in_specs=[in_smem(), in_smem()] + [in_vmem()] * 5,
        out_specs=(in_vmem(),) * 4,
        scratch_shapes=[pltpu.VMEM((2, 8, 512), jnp.float32)],
        compiler_params=settings(8),
        cost_estimate=pl.CostEstimate(flops=10**8, bytes_accessed=10**6, transcendentals=0),
        name="upward",
    )(domain, half_widths, point_coords, strengths, const, centers, half_widths[None, :])

    parts = pl.pallas_call(
        tile_kernel,
        out_shape=jax.ShapeDtypeStruct((DOMAINS * 12, 1, 128), jnp.float32),
        in_specs=[in_vmem()] * 4,
        out_specs=in_vmem(),
        scratch_shapes=[
            pltpu.SMEM((DOMAINS + 8,), jnp.int32),
            pltpu.SMEM((8, 128), jnp.int32),
            pltpu.SMEM((16, 128), jnp.float32),
            pltpu.VMEM((8, 128), jnp.int32),
            pltpu.VMEM((16, 128), jnp.float32),
            pltpu.SemaphoreType.DMA((2,)),
        ],
        compiler_params=settings(8),
        name="tiles",
    )(received, own_places, features, kept_const)

    relayed = exchange(parts.reshape(DOMAINS, 1, 1536))
    ordered = pl.pallas_call(
        relay_kernel,
        out_shape=jax.ShapeDtypeStruct((DOMAINS * 12, 128), jnp.float32),
        in_specs=[in_vmem()] * 2,
        out_specs=in_vmem(),
        compiler_params=settings(4),
        name="relay",
    )(owners, relayed.reshape(DOMAINS * 12, 128))
    arrived = exchange(ordered.reshape(DOMAINS, 1, 1536))

    return pl.pallas_call(
        downward_kernel,
        out_shape=jax.ShapeDtypeStruct((3, CL_DEV * PTS), jnp.float32),
        in_specs=[in_vmem(), in_vmem(), in_vmem()],
        out_specs=pl.BlockSpec(memory_space=pl.ANY),
        scratch_shapes=[
            pltpu.VMEM((12 * CL_DEV, 128), jnp.float32),
            pltpu.VMEM((3, CL_DEV * PTS), jnp.float32),
            pltpu.SemaphoreType.DMA((CL_DEV // 4,)),
        ],
        compiler_params=settings(8),
        name="downward",
    )(received, arrived.reshape(DOMAINS * 12, 128), basis)


def solution(mesh):
    return jax.shard_map(
        local,
        mesh=mesh,
        in_specs=(
            P(None, AXES),
            P(None, AXES),
            P(),
            P(),
            P(AXES, None),
            P(AXES, None),
            P(AXES),
        ),
        out_specs=P(None, AXES),
        check_vma=False,
    )
```

```python
import functools
import math

import jax
import jax.numpy as jnp
import numpy as np
from jax import lax
from jax.experimental import pallas as pl
from jax.experimental.pallas import tpu as pltpu
from jax.sharding import PartitionSpec as P

CL_DEV = 16
PTS = 1024
DEG = 7
TILES_DEV = 128
DOMAINS = 128
NODES = DEG + 1
GROUPS = (16, 8, 4, 2, 1)
AXES = ("gx", "gy")

smoothing_sq = 0.01
biot_factor = -0.07957747154594767

node_values = np.cos(np.pi * np.arange(NODES) / DEG)
node_list = [float(v) for v in node_values.astype(np.float32)]
node_scales = [
    1.0 / math.prod(node_list[a] - node_list[m] for m in range(NODES) if m != a)
    for a in range(NODES)
]


def build_constants():
    nodes = node_values.astype(np.float32)
    lane = np.arange(128)
    table = np.zeros((8, 8, 128), np.float32)
    for group in range(4):
        table[group] = nodes[group + 4 * (lane // 64)][None, :]
    table[4] = nodes[(lane // 8) % 8][None, :]
    table[5] = nodes[lane % 8][None, :]
    table[6] = nodes[:, None]
    table[7, :4] = table[:4, 0]
    return table


CONSTANTS = build_constants()


def split_bf16(value):
    high = value.astype(jnp.bfloat16)
    return high, (value - high.astype(jnp.float32)).astype(jnp.bfloat16)


def lagrange_rows(row, sublane):
    spread = jnp.broadcast_to(row, (NODES, row.shape[1]))
    result = None
    for m in range(NODES):
        factor = jnp.where(sublane == m, node_scales[m], spread - node_list[m])
        result = factor if result is None else result * factor
    return result


def paired_rows(basis_y, basis_z):
    return jnp.concatenate([basis_y[b : b + 1] * basis_z for b in range(NODES)], axis=0)


def split_exactly(value):
    high = value.astype(jnp.bfloat16)
    rest = value - high.astype(jnp.float32)
    middle = rest.astype(jnp.bfloat16)
    return high, middle, (rest - middle.astype(jnp.float32)).astype(jnp.bfloat16)


def message_kernel(count_ref, source_ref, target_ref, center_ref, width_ref, out_ref, owner_ref):
    slot = lax.broadcasted_iota(jnp.int32, (DOMAINS, TILES_DEV), 0)
    lane = lax.broadcasted_iota(jnp.int32, (1, TILES_DEV), 1)
    alive = lane < count_ref[0]
    source = jnp.where(alive, source_ref[...], -1)
    target = jnp.where(alive, target_ref[...], -1)
    owner_ref[0:1] = source >> 4
    owner_ref[1:2] = target >> 4
    from_source = jnp.where(slot == source >> 4, 1.0, 0.0).astype(jnp.bfloat16)
    from_target = jnp.where(slot == target >> 4, 1.0, 0.0).astype(jnp.bfloat16)
    clusters = center_ref.shape[1]
    number = lax.broadcasted_iota(jnp.int32, (clusters, TILES_DEV), 0)
    chosen = jnp.where(number == target, 1.0, 0.0).astype(jnp.bfloat16)
    places = jnp.concatenate([center_ref[...], width_ref[...], jnp.zeros((4, clusters))], axis=0)
    terms = jnp.concatenate(split_exactly(places), axis=0)
    rows = jnp.dot(terms, chosen, preferred_element_type=jnp.float32)
    row = lax.broadcasted_iota(jnp.int32, (24, TILES_DEV), 0)
    local_source = ((source & 15) + 1).astype(jnp.float32)
    local_target = ((target & 15) + 1).astype(jnp.float32)
    rows = jnp.where(row == 4, local_source, rows)
    spread = functools.partial(
        lax.dot_general,
        dimension_numbers=(((1,), (1,)), ((), ())),
        preferred_element_type=jnp.float32,
    )
    out_ref[:, 0:24] = spread(from_source, rows.astype(jnp.bfloat16)) + spread(
        from_target, jnp.where(row == 5, local_target, 0.0).astype(jnp.bfloat16)
    )


def upward_kernel(domain_ref, width_ref, coord_ref, strength_ref, const_ref, center_ref, all_width_ref, feature_ref, own_ref, same_ref, basis_ref, rows_ref):
    same_ref[...] = const_ref[...]
    domain = domain_ref[0]
    nearby = pl.ds(pl.multiple_of((domain >> 3) * 128, 128), 128)
    places = jnp.concatenate(
        [center_ref[:, nearby], all_width_ref[:, nearby], jnp.zeros((4, 128))], axis=0
    )
    own_ref[...] = pltpu.roll(places, 128 - (domain & 7) * CL_DEV, 1)
    sublane = lax.broadcasted_iota(jnp.int32, (NODES, PTS), 0)
    lane = lax.broadcasted_iota(jnp.int32, (8, 128), 1)

    def one_cluster(cluster, rows):
        where = pl.ds(pl.multiple_of(cluster * PTS, PTS), PTS)
        basis = [lagrange_rows(coord_ref[axis : axis + 1, where], sublane) for axis in range(3)]
        for axis in range(3):
            basis_ref[8 * axis : 8 * axis + 8, where] = basis[axis]
        paired = paired_rows(basis[1], basis[2])
        weighted = jnp.concatenate(
            [strength_ref[c : c + 1, where] * basis[0] for c in range(3)], axis=0
        )
        paired_high, paired_low = split_bf16(paired)
        weighted_high, weighted_low = split_bf16(weighted)
        left = jnp.concatenate([weighted_high, weighted_low], axis=0)
        contract = functools.partial(
            lax.dot_general,
            dimension_numbers=(((1,), (1,)), ((), ())),
            preferred_element_type=jnp.float32,
        )
        twice_high = jnp.concatenate([paired_high, paired_high], axis=0)
        twice_low = jnp.concatenate([paired_low, paired_low], axis=0)
        by_high = contract(left, twice_high)
        by_low = contract(weighted_high, twice_low)
        charge = by_high[:24] + by_high[24:] + by_low
        charge = charge * biot_factor
        charges = []
        for c in range(3):
            block = charge[8 * c : 8 * c + 8]
            moved = jnp.concatenate([block[4:], block[:4]], axis=0)
            charges.append(jnp.where(lane < 64, block, moved))
        width = width_ref[domain * CL_DEV + cluster]
        node_x = const_ref[7] * width
        node_y = const_ref[4] * width
        node_z = const_ref[5] * width
        moments = [
            node_y * charges[2] - node_z * charges[1],
            node_z * charges[0] - node_x * charges[2],
            node_x * charges[1] - node_y * charges[0],
        ]
        order = [charges[0], charges[1], charges[2], charges[0], charges[1]] + moments
        for row, value in enumerate(order):
            for group in range(4):
                rows[row : row + 1, 128 * group : 128 * group + 128] = value[group : group + 1]
        high, low = split_bf16(rows[...])
        feature_ref[cluster] = jnp.concatenate([high, low], axis=0)

    @pl.loop(0, CL_DEV, step=2)
    def _(cluster):
        for extra in range(2):
            one_cluster(cluster + extra, rows_ref.at[extra])


def kernel_blocks(width, target_x, square_yz, group_pair, lane_pair):
    highs, lows = [], []
    for lanes in (2 * lane_pair, 2 * lane_pair + 1):
        high_rows, low_rows = [], []
        for group in (2 * group_pair, 2 * group_pair + 1):
            for half in range(2):
                apart_x = target_x[lanes] - width * node_list[group + 4 * half]
                square_x = apart_x * apart_x
                for b in range(0, NODES, 2):
                    pair = []
                    for square in square_yz[b : b + 2]:
                        inverse = lax.rsqrt(square + square_x)
                        pair.append(inverse * inverse * inverse)
                    high, low = split_bf16(jnp.concatenate(pair, axis=0))
                    high_rows.append(high)
                    low_rows.append(low)
        highs.append(jnp.concatenate(high_rows, axis=0))
        lows.append(jnp.concatenate(low_rows, axis=0))
    return jnp.concatenate(highs, axis=1), jnp.concatenate(lows, axis=1)


def tile_kernel(request_ref, own_ref, feature_ref, const_ref, out_ref, order_ref, number_ref, place_ref, number_vmem, place_vmem, semaphore):
    sublane = lax.broadcasted_iota(jnp.int32, (8, 128), 0)
    request = request_ref[...].T
    request = request[0:8] + request[8:16] + request[16:24]
    number_vmem[...] = request.astype(jnp.int32)
    place_vmem[0:8] = request
    place_vmem[8:16] = own_ref[...]
    copies = [
        pltpu.make_async_copy(number_vmem, number_ref, semaphore.at[0]),
        pltpu.make_async_copy(place_vmem, place_ref, semaphore.at[1]),
    ]
    for copy in copies:
        copy.start()
    for copy in copies:
        copy.wait()

    total = 0
    for peer in range(DOMAINS):
        order_ref[total] = peer
        total += (number_ref[4, peer] > 0).astype(jnp.int32)
    order_ref[total] = order_ref[jnp.maximum(total - 1, 0)]
    padded = total + (total % 4 == 3).astype(jnp.int32)

    def one_tile(peer):
        local_id = number_ref[4, peer] - 1
        source_width = place_ref[11, local_id]
        target_width = place_ref[3, peer]
        shift = [place_ref[axis, peer] - place_ref[8 + axis, local_id] for axis in range(3)]
        target_x = [const_ref[group] * target_width + shift[0] for group in range(4)]
        target_y = const_ref[4] * target_width + shift[1]
        target_z = const_ref[5] * target_width + shift[2]
        apart_z = target_z - const_ref[6] * source_width
        square_z = apart_z * apart_z + smoothing_sq
        square_yz = []
        for b in range(NODES):
            apart_y = target_y - source_width * node_list[b]
            square_yz.append(square_z + apart_y * apart_y)
        feature = feature_ref[local_id]
        first_rows = jnp.where(sublane == 0, target_y, target_z)
        second_rows = jnp.where(sublane == 0, target_z, target_y)
        for lane_pair in range(2):
            summed = None
            for group_pair in range(2):
                columns = feature[:, 256 * group_pair : 256 * group_pair + 256]
                for block in kernel_blocks(
                    source_width, target_x, square_yz, group_pair, lane_pair
                ):
                    product = jnp.dot(columns, block, preferred_element_type=jnp.float32)
                    summed = product if summed is None else summed + product
            summed = summed[:8] + summed[8:]
            for side in range(2):
                lanes = 2 * lane_pair + side
                block = summed[:, 128 * side : 128 * side + 128]
                first = jnp.where(sublane < 2, first_rows, target_x[lanes])
                second = jnp.where(sublane == 1, target_x[lanes], second_rows)
                velocity = (
                    first * pltpu.roll(block, 6, 0)
                    - second * pltpu.roll(block, 7, 0)
                    - pltpu.roll(block, 3, 0)
                )
                for c in range(3):
                    out_ref[peer * 12 + c * 4 + lanes] = velocity[c : c + 1]

    done = 0
    for size in GROUPS:
        rounds = (padded - done) // size

        @pl.loop(0, rounds)
        def _(step):
            for extra in range(size):
                one_tile(order_ref[done + step * size + extra])

        done += rounds * size


def relay_kernel(owner_ref, in_ref, out_ref):
    slot = lax.broadcasted_iota(jnp.int32, (DOMAINS, TILES_DEV), 0)
    from_source = jnp.where(slot == owner_ref[0:1], 1.0, 0.0).astype(jnp.bfloat16)
    from_target = jnp.where(slot == owner_ref[1:2], 1.0, 0.0).astype(jnp.bfloat16)
    order = lax.dot_general(
        from_target, from_source, (((1,), (1,)), ((), ())), preferred_element_type=jnp.float32
    ).astype(jnp.bfloat16)
    arrived = jnp.dot(
        from_source, jnp.ones((TILES_DEV, 128), jnp.bfloat16), preferred_element_type=jnp.float32
    )
    alive = arrived > 0.5
    for chunk in range(12):
        rows = pl.ds(chunk, DOMAINS, stride=12)
        moved = None
        for term in split_exactly(jnp.where(alive, in_ref[rows, :], 0.0)):
            product = jnp.dot(order, term, preferred_element_type=jnp.float32)
            moved = product if moved is None else moved + product
        out_ref[rows, :] = moved


def downward_kernel(owner_ref, part_ref, basis_ref, out_ref, proxy_ref, held_ref, semaphore):
    owner = owner_ref[:, 5:6].astype(jnp.int32)
    column = lax.broadcasted_iota(jnp.int32, (DOMAINS, CL_DEV), 1)
    assign = (owner == column + 1).astype(jnp.bfloat16)
    gather = functools.partial(
        lax.dot_general,
        dimension_numbers=(((0,), (0,)), ((), ())),
        preferred_element_type=jnp.float32,
    )
    for chunk in range(12):
        high, low = split_bf16(part_ref[pl.ds(chunk, DOMAINS, stride=12), :])
        proxy_ref[chunk * CL_DEV : (chunk + 1) * CL_DEV] = gather(assign, high) + gather(
            assign, low
        )

    def one_cluster(cluster):
        where = pl.ds(cluster * PTS, PTS)
        rows = proxy_ref[pl.ds(cluster, 12, stride=CL_DEV), :]
        near, far = rows[:, :64], rows[:, 64:]
        left = jnp.concatenate(
            [piece[4 * c : 4 * c + 4] for c in range(3) for piece in (near, far)], axis=0
        )
        left_high, left_low = split_bf16(left)
        paired_high, paired_low = split_bf16(
            paired_rows(basis_ref[8:16, where], basis_ref[16:24, where])
        )
        spread = jnp.dot(
            jnp.concatenate([left_high, left_low, left_high], axis=1),
            jnp.concatenate([paired_high, paired_high, paired_low], axis=0),
            preferred_element_type=jnp.float32,
        )
        basis_x = basis_ref[0:8, where]
        for c in range(3):
            held_ref[c : c + 1, where] = jnp.sum(
                spread[8 * c : 8 * c + 8] * basis_x, axis=0, keepdims=True
            )

    copies = []
    for cluster in range(CL_DEV):
        one_cluster(cluster)
        if cluster % 4 == 3:
            where = pl.ds((cluster - 3) * PTS, 4 * PTS)
            copies.append(
                pltpu.make_async_copy(
                    held_ref.at[:, where], out_ref.at[:, where], semaphore.at[cluster // 4]
                )
            )
            copies[-1].start()
    for copy in copies:
        copy.wait()


def in_vmem():
    return pl.BlockSpec(memory_space=pltpu.VMEM)


def in_smem():
    return pl.BlockSpec(memory_space=pltpu.SMEM)


def exchange(value):
    return lax.all_to_all(value, AXES, split_axis=0, concat_axis=0, tiled=True)


def settings(mebibytes):
    return pltpu.CompilerParams(vmem_limit_bytes=mebibytes << 20)


def local(point_coords, strengths, centers, half_widths, tile_source, tile_target, tile_count):
    domain = lax.axis_index(AXES).reshape(1)
    const = jnp.asarray(CONSTANTS)
    message, owners = pl.pallas_call(
        message_kernel,
        out_shape=(
            jax.ShapeDtypeStruct((DOMAINS, 128), jnp.float32),
            jax.ShapeDtypeStruct((2, TILES_DEV), jnp.int32),
        ),
        in_specs=[in_smem()] + [in_vmem()] * 4,
        out_specs=(in_vmem(), in_vmem()),
        name="message",
    )(tile_count, tile_source, tile_target, centers, half_widths[None, :])
    received = exchange(message.reshape(DOMAINS, 1, 128)).reshape(DOMAINS, 128)

    features, own_places, kept_const, basis = pl.pallas_call(
        upward_kernel,
        out_shape=(
            jax.ShapeDtypeStruct((CL_DEV, 16, 512), jnp.bfloat16),
            jax.ShapeDtypeStruct((8, 128), jnp.float32),
            jax.ShapeDtypeStruct(const.shape, jnp.float32),
            jax.ShapeDtypeStruct((24, CL_DEV * PTS), jnp.float32),
        ),
        in_specs=[in_smem(), in_smem()] + [in_vmem()] * 5,
        out_specs=(in_vmem(),) * 4,
        scratch_shapes=[pltpu.VMEM((2, 8, 512), jnp.float32)],
        compiler_params=settings(8),
        cost_estimate=pl.CostEstimate(flops=10**8, bytes_accessed=10**6, transcendentals=0),
        name="upward",
    )(domain, half_widths, point_coords, strengths, const, centers, half_widths[None, :])

    parts = pl.pallas_call(
        tile_kernel,
        out_shape=jax.ShapeDtypeStruct((DOMAINS * 12, 1, 128), jnp.float32),
        in_specs=[in_vmem()] * 4,
        out_specs=in_vmem(),
        scratch_shapes=[
            pltpu.SMEM((DOMAINS + 8,), jnp.int32),
            pltpu.SMEM((8, 128), jnp.int32),
            pltpu.SMEM((16, 128), jnp.float32),
            pltpu.VMEM((8, 128), jnp.int32),
            pltpu.VMEM((16, 128), jnp.float32),
            pltpu.SemaphoreType.DMA((2,)),
        ],
        compiler_params=settings(8),
        name="tiles",
    )(received, own_places, features, kept_const)

    relayed = exchange(parts.reshape(DOMAINS, 1, 1536))
    ordered = pl.pallas_call(
        relay_kernel,
        out_shape=jax.ShapeDtypeStruct((DOMAINS * 12, 128), jnp.float32),
        in_specs=[in_vmem()] * 2,
        out_specs=in_vmem(),
        compiler_params=settings(4),
        name="relay",
    )(owners, relayed.reshape(DOMAINS * 12, 128))
    arrived = exchange(ordered.reshape(DOMAINS, 1, 1536))

    return pl.pallas_call(
        downward_kernel,
        out_shape=jax.ShapeDtypeStruct((3, CL_DEV * PTS), jnp.float32),
        in_specs=[in_vmem(), in_vmem(), in_vmem()],
        out_specs=pl.BlockSpec(memory_space=pl.ANY),
        scratch_shapes=[
            pltpu.VMEM((12 * CL_DEV, 128), jnp.float32),
            pltpu.VMEM((3, CL_DEV * PTS), jnp.float32),
            pltpu.SemaphoreType.DMA((CL_DEV // 4,)),
        ],
        compiler_params=settings(8),
        name="downward",
    )(received, arrived.reshape(DOMAINS * 12, 128), basis)


def solution(mesh):
    return jax.shard_map(
        local,
        mesh=mesh,
        in_specs=(
            P(None, AXES),
            P(None, AXES),
            P(),
            P(),
            P(AXES, None),
            P(AXES, None),
            P(AXES),
        ),
        out_specs=P(None, AXES),
        check_vma=False,
    )
```

```python
import functools
import math

import jax
import jax.numpy as jnp
import numpy as np
from jax import lax
from jax.experimental import pallas as pl
from jax.experimental.pallas import tpu as pltpu
from jax.sharding import PartitionSpec as P

CL_DEV = 16
PTS = 1024
DEG = 7
TILES_DEV = 128
DOMAINS = 128
NODES = DEG + 1
GROUPS = (16, 8, 4, 2, 1)
AXES = ("gx", "gy")

smoothing_sq = 0.01
biot_factor = -0.07957747154594767

node_values = np.cos(np.pi * np.arange(NODES) / DEG)
node_list = [float(v) for v in node_values.astype(np.float32)]
node_scales = [
    1.0 / math.prod(node_list[a] - node_list[m] for m in range(NODES) if m != a)
    for a in range(NODES)
]


def build_constants():
    nodes = node_values.astype(np.float32)
    lane = np.arange(128)
    table = np.zeros((8, 8, 128), np.float32)
    for group in range(4):
        table[group] = nodes[group + 4 * (lane // 64)][None, :]
    table[4] = nodes[(lane // 8) % 8][None, :]
    table[5] = nodes[lane % 8][None, :]
    table[6] = nodes[:, None]
    table[7, :4] = table[:4, 0]
    return table


CONSTANTS = build_constants()


def split_bf16(value):
    high = value.astype(jnp.bfloat16)
    return high, (value - high.astype(jnp.float32)).astype(jnp.bfloat16)


def lagrange_rows(row, sublane):
    spread = jnp.broadcast_to(row, (NODES, row.shape[1]))
    result = None
    for m in range(NODES):
        factor = jnp.where(sublane == m, node_scales[m], spread - node_list[m])
        result = factor if result is None else result * factor
    return result


def paired_rows(basis_y, basis_z):
    return jnp.concatenate([basis_y[b : b + 1] * basis_z for b in range(NODES)], axis=0)


def split_exactly(value):
    high = value.astype(jnp.bfloat16)
    rest = value - high.astype(jnp.float32)
    middle = rest.astype(jnp.bfloat16)
    return high, middle, (rest - middle.astype(jnp.float32)).astype(jnp.bfloat16)


def message_kernel(count_ref, source_ref, target_ref, center_ref, width_ref, out_ref, owner_ref):
    slot = lax.broadcasted_iota(jnp.int32, (DOMAINS, TILES_DEV), 0)
    lane = lax.broadcasted_iota(jnp.int32, (1, TILES_DEV), 1)
    alive = lane < count_ref[0]
    source = jnp.where(alive, source_ref[...], -1)
    target = jnp.where(alive, target_ref[...], -1)
    owner_ref[0:1] = source >> 4
    owner_ref[1:2] = target >> 4
    from_source = jnp.where(slot == source >> 4, 1.0, 0.0).astype(jnp.bfloat16)
    from_target = jnp.where(slot == target >> 4, 1.0, 0.0).astype(jnp.bfloat16)
    clusters = center_ref.shape[1]
    number = lax.broadcasted_iota(jnp.int32, (clusters, TILES_DEV), 0)
    chosen = jnp.where(number == target, 1.0, 0.0).astype(jnp.bfloat16)
    places = jnp.concatenate([center_ref[...], width_ref[...], jnp.zeros((4, clusters))], axis=0)
    terms = jnp.concatenate(split_exactly(places), axis=0)
    rows = jnp.dot(terms, chosen, preferred_element_type=jnp.float32)
    row = lax.broadcasted_iota(jnp.int32, (24, TILES_DEV), 0)
    local_source = ((source & 15) + 1).astype(jnp.float32)
    local_target = ((target & 15) + 1).astype(jnp.float32)
    rows = jnp.where(row == 4, local_source, rows)
    spread = functools.partial(
        lax.dot_general,
        dimension_numbers=(((1,), (1,)), ((), ())),
        preferred_element_type=jnp.float32,
    )
    out_ref[:, 0:24] = spread(from_source, rows.astype(jnp.bfloat16)) + spread(
        from_target, jnp.where(row == 5, local_target, 0.0).astype(jnp.bfloat16)
    )


def upward_kernel(domain_ref, width_ref, coord_ref, strength_ref, const_ref, center_ref, all_width_ref, feature_ref, own_ref, same_ref, basis_ref, rows_ref):
    same_ref[...] = const_ref[...]
    domain = domain_ref[0]
    nearby = pl.ds(pl.multiple_of((domain >> 3) * 128, 128), 128)
    places = jnp.concatenate(
        [center_ref[:, nearby], all_width_ref[:, nearby], jnp.zeros((4, 128))], axis=0
    )
    own_ref[...] = pltpu.roll(places, 128 - (domain & 7) * CL_DEV, 1)
    sublane = lax.broadcasted_iota(jnp.int32, (NODES, PTS), 0)
    lane = lax.broadcasted_iota(jnp.int32, (8, 128), 1)

    def one_cluster(cluster, rows):
        where = pl.ds(pl.multiple_of(cluster * PTS, PTS), PTS)
        basis = [lagrange_rows(coord_ref[axis : axis + 1, where], sublane) for axis in range(3)]
        for axis in range(3):
            basis_ref[8 * axis : 8 * axis + 8, where] = basis[axis]
        paired = paired_rows(basis[1], basis[2])
        weighted = jnp.concatenate(
            [strength_ref[c : c + 1, where] * basis[0] for c in range(3)], axis=0
        )
        paired_high, paired_low = split_bf16(paired)
        weighted_high, weighted_low = split_bf16(weighted)
        left = jnp.concatenate([weighted_high, weighted_low], axis=0)
        contract = functools.partial(
            lax.dot_general,
            dimension_numbers=(((1,), (1,)), ((), ())),
            preferred_element_type=jnp.float32,
        )
        twice_high = jnp.concatenate([paired_high, paired_high], axis=0)
        twice_low = jnp.concatenate([paired_low, paired_low], axis=0)
        by_high = contract(left, twice_high)
        by_low = contract(weighted_high, twice_low)
        charge = by_high[:24] + by_high[24:] + by_low
        charge = charge * biot_factor
        charges = []
        for c in range(3):
            block = charge[8 * c : 8 * c + 8]
            moved = jnp.concatenate([block[4:], block[:4]], axis=0)
            charges.append(jnp.where(lane < 64, block, moved))
        width = width_ref[domain * CL_DEV + cluster]
        node_x = const_ref[7] * width
        node_y = const_ref[4] * width
        node_z = const_ref[5] * width
        moments = [
            node_y * charges[2] - node_z * charges[1],
            node_z * charges[0] - node_x * charges[2],
            node_x * charges[1] - node_y * charges[0],
        ]
        order = [charges[0], charges[1], charges[2], charges[0], charges[1]] + moments
        for row, value in enumerate(order):
            for group in range(4):
                rows[row : row + 1, 128 * group : 128 * group + 128] = value[group : group + 1]
        high, low = split_bf16(rows[...])
        feature_ref[cluster] = jnp.concatenate([high, low], axis=0)

    @pl.loop(0, CL_DEV, step=2)
    def _(cluster):
        for extra in range(2):
            one_cluster(cluster + extra, rows_ref.at[extra])


def kernel_blocks(width, target_x, square_yz, group_pair, lane_pair):
    highs, lows = [], []
    for lanes in (2 * lane_pair, 2 * lane_pair + 1):
        high_rows, low_rows = [], []
        for group in (2 * group_pair, 2 * group_pair + 1):
            for half in range(2):
                apart_x = target_x[lanes] - width * node_list[group + 4 * half]
                square_x = apart_x * apart_x
                for b in range(0, NODES, 2):
                    pair = []
                    for square in square_yz[b : b + 2]:
                        inverse = lax.rsqrt(square + square_x)
                        pair.append(inverse * inverse * inverse)
                    high, low = split_bf16(jnp.concatenate(pair, axis=0))
                    high_rows.append(high)
                    low_rows.append(low)
        highs.append(jnp.concatenate(high_rows, axis=0))
        lows.append(jnp.concatenate(low_rows, axis=0))
    return jnp.concatenate(highs, axis=1), jnp.concatenate(lows, axis=1)


def tile_kernel(request_ref, own_ref, feature_ref, const_ref, out_ref, order_ref, number_ref, place_ref, number_vmem, place_vmem, semaphore):
    sublane = lax.broadcasted_iota(jnp.int32, (8, 128), 0)
    request = request_ref[...].T
    request = request[0:8] + request[8:16] + request[16:24]
    number_vmem[...] = request.astype(jnp.int32)
    place_vmem[0:8] = request
    place_vmem[8:16] = own_ref[...]
    copies = [
        pltpu.make_async_copy(number_vmem, number_ref, semaphore.at[0]),
        pltpu.make_async_copy(place_vmem, place_ref, semaphore.at[1]),
    ]
    for copy in copies:
        copy.start()
    for copy in copies:
        copy.wait()

    total = 0
    for peer in range(DOMAINS):
        order_ref[total] = peer
        total += (number_ref[4, peer] > 0).astype(jnp.int32)
    order_ref[total] = order_ref[jnp.maximum(total - 1, 0)]
    padded = total + (total % 4 == 3).astype(jnp.int32)

    def one_tile(peer):
        local_id = number_ref[4, peer] - 1
        source_width = place_ref[11, local_id]
        target_width = place_ref[3, peer]
        shift = [place_ref[axis, peer] - place_ref[8 + axis, local_id] for axis in range(3)]
        target_x = [const_ref[group] * target_width + shift[0] for group in range(4)]
        target_y = const_ref[4] * target_width + shift[1]
        target_z = const_ref[5] * target_width + shift[2]
        apart_z = target_z - const_ref[6] * source_width
        square_z = apart_z * apart_z + smoothing_sq
        square_yz = []
        for b in range(NODES):
            apart_y = target_y - source_width * node_list[b]
            square_yz.append(square_z + apart_y * apart_y)
        feature = feature_ref[local_id]
        first_rows = jnp.where(sublane == 0, target_y, target_z)
        second_rows = jnp.where(sublane == 0, target_z, target_y)
        for lane_pair in range(2):
            summed = None
            for group_pair in range(2):
                columns = feature[:, 256 * group_pair : 256 * group_pair + 256]
                for block in kernel_blocks(
                    source_width, target_x, square_yz, group_pair, lane_pair
                ):
                    product = jnp.dot(columns, block, preferred_element_type=jnp.float32)
                    summed = product if summed is None else summed + product
            summed = summed[:8] + summed[8:]
            for side in range(2):
                lanes = 2 * lane_pair + side
                block = summed[:, 128 * side : 128 * side + 128]
                first = jnp.where(sublane < 2, first_rows, target_x[lanes])
                second = jnp.where(sublane == 1, target_x[lanes], second_rows)
                velocity = (
                    first * pltpu.roll(block, 6, 0)
                    - second * pltpu.roll(block, 7, 0)
                    - pltpu.roll(block, 3, 0)
                )
                for c in range(3):
                    out_ref[peer * 12 + c * 4 + lanes] = velocity[c : c + 1]

    done = 0
    for size in GROUPS:
        rounds = (padded - done) // size

        @pl.loop(0, rounds)
        def _(step):
            for extra in range(size):
                one_tile(order_ref[done + step * size + extra])

        done += rounds * size


def relay_kernel(owner_ref, in_ref, out_ref):
    slot = lax.broadcasted_iota(jnp.int32, (DOMAINS, TILES_DEV), 0)
    from_source = jnp.where(slot == owner_ref[0:1], 1.0, 0.0).astype(jnp.bfloat16)
    from_target = jnp.where(slot == owner_ref[1:2], 1.0, 0.0).astype(jnp.bfloat16)
    order = lax.dot_general(
        from_target, from_source, (((1,), (1,)), ((), ())), preferred_element_type=jnp.float32
    ).astype(jnp.bfloat16)
    arrived = jnp.dot(
        from_source, jnp.ones((TILES_DEV, 128), jnp.bfloat16), preferred_element_type=jnp.float32
    )
    alive = arrived > 0.5
    for chunk in range(12):
        rows = pl.ds(chunk, DOMAINS, stride=12)
        moved = None
        for term in split_bf16(jnp.where(alive, in_ref[rows, :], 0.0)):
            product = jnp.dot(order, term, preferred_element_type=jnp.float32)
            moved = product if moved is None else moved + product
        out_ref[rows, :] = moved


def downward_kernel(owner_ref, part_ref, basis_ref, out_ref, proxy_ref, held_ref, semaphore):
    owner = owner_ref[:, 5:6].astype(jnp.int32)
    column = lax.broadcasted_iota(jnp.int32, (DOMAINS, CL_DEV), 1)
    assign = (owner == column + 1).astype(jnp.bfloat16)
    gather = functools.partial(
        lax.dot_general,
        dimension_numbers=(((0,), (0,)), ((), ())),
        preferred_element_type=jnp.float32,
    )
    for chunk in range(12):
        high, low = split_bf16(part_ref[pl.ds(chunk, DOMAINS, stride=12), :])
        proxy_ref[chunk * CL_DEV : (chunk + 1) * CL_DEV] = gather(assign, high) + gather(
            assign, low
        )

    def one_cluster(cluster):
        where = pl.ds(cluster * PTS, PTS)
        rows = proxy_ref[pl.ds(cluster, 12, stride=CL_DEV), :]
        near, far = rows[:, :64], rows[:, 64:]
        left = jnp.concatenate(
            [piece[4 * c : 4 * c + 4] for c in range(3) for piece in (near, far)], axis=0
        )
        left_high, left_low = split_bf16(left)
        paired_high, paired_low = split_bf16(
            paired_rows(basis_ref[8:16, where], basis_ref[16:24, where])
        )
        spread = jnp.dot(
            jnp.concatenate([left_high, left_low, left_high], axis=1),
            jnp.concatenate([paired_high, paired_high, paired_low], axis=0),
            preferred_element_type=jnp.float32,
        )
        basis_x = basis_ref[0:8, where]
        for c in range(3):
            held_ref[c : c + 1, where] = jnp.sum(
                spread[8 * c : 8 * c + 8] * basis_x, axis=0, keepdims=True
            )

    copies = []
    for cluster in range(CL_DEV):
        one_cluster(cluster)
        if cluster % 4 == 3:
            where = pl.ds((cluster - 3) * PTS, 4 * PTS)
            copies.append(
                pltpu.make_async_copy(
                    held_ref.at[:, where], out_ref.at[:, where], semaphore.at[cluster // 4]
                )
            )
            copies[-1].start()
    for copy in copies:
        copy.wait()


def in_vmem():
    return pl.BlockSpec(memory_space=pltpu.VMEM)


def in_smem():
    return pl.BlockSpec(memory_space=pltpu.SMEM)


def exchange(value):
    return lax.all_to_all(value, AXES, split_axis=0, concat_axis=0, tiled=True)


def settings(mebibytes):
    return pltpu.CompilerParams(vmem_limit_bytes=mebibytes << 20)


def local(point_coords, strengths, centers, half_widths, tile_source, tile_target, tile_count):
    domain = lax.axis_index(AXES).reshape(1)
    const = jnp.asarray(CONSTANTS)
    message, owners = pl.pallas_call(
        message_kernel,
        out_shape=(
            jax.ShapeDtypeStruct((DOMAINS, 128), jnp.float32),
            jax.ShapeDtypeStruct((2, TILES_DEV), jnp.int32),
        ),
        in_specs=[in_smem()] + [in_vmem()] * 4,
        out_specs=(in_vmem(), in_vmem()),
        name="message",
    )(tile_count, tile_source, tile_target, centers, half_widths[None, :])
    received = exchange(message.reshape(DOMAINS, 1, 128)).reshape(DOMAINS, 128)

    features, own_places, kept_const, basis = pl.pallas_call(
        upward_kernel,
        out_shape=(
            jax.ShapeDtypeStruct((CL_DEV, 16, 512), jnp.bfloat16),
            jax.ShapeDtypeStruct((8, 128), jnp.float32),
            jax.ShapeDtypeStruct(const.shape, jnp.float32),
            jax.ShapeDtypeStruct((24, CL_DEV * PTS), jnp.float32),
        ),
        in_specs=[in_smem(), in_smem()] + [in_vmem()] * 5,
        out_specs=(in_vmem(),) * 4,
        scratch_shapes=[pltpu.VMEM((2, 8, 512), jnp.float32)],
        compiler_params=settings(8),
        cost_estimate=pl.CostEstimate(flops=10**8, bytes_accessed=10**6, transcendentals=0),
        name="upward",
    )(domain, half_widths, point_coords, strengths, const, centers, half_widths[None, :])

    parts = pl.pallas_call(
        tile_kernel,
        out_shape=jax.ShapeDtypeStruct((DOMAINS * 12, 1, 128), jnp.float32),
        in_specs=[in_vmem()] * 4,
        out_specs=in_vmem(),
        scratch_shapes=[
            pltpu.SMEM((DOMAINS + 8,), jnp.int32),
            pltpu.SMEM((8, 128), jnp.int32),
            pltpu.SMEM((16, 128), jnp.float32),
            pltpu.VMEM((8, 128), jnp.int32),
            pltpu.VMEM((16, 128), jnp.float32),
            pltpu.SemaphoreType.DMA((2,)),
        ],
        compiler_params=settings(8),
        name="tiles",
    )(received, own_places, features, kept_const)

    relayed = exchange(parts.reshape(DOMAINS, 1, 1536))
    ordered = pl.pallas_call(
        relay_kernel,
        out_shape=jax.ShapeDtypeStruct((DOMAINS * 12, 128), jnp.float32),
        in_specs=[in_vmem()] * 2,
        out_specs=in_vmem(),
        compiler_params=settings(4),
        name="relay",
    )(owners, relayed.reshape(DOMAINS * 12, 128))
    arrived = exchange(ordered.reshape(DOMAINS, 1, 1536))

    return pl.pallas_call(
        downward_kernel,
        out_shape=jax.ShapeDtypeStruct((3, CL_DEV * PTS), jnp.float32),
        in_specs=[in_vmem(), in_vmem(), in_vmem()],
        out_specs=pl.BlockSpec(memory_space=pl.ANY),
        scratch_shapes=[
            pltpu.VMEM((12 * CL_DEV, 128), jnp.float32),
            pltpu.VMEM((3, CL_DEV * PTS), jnp.float32),
            pltpu.SemaphoreType.DMA((CL_DEV // 4,)),
        ],
        compiler_params=settings(8),
        name="downward",
    )(received, arrived.reshape(DOMAINS * 12, 128), basis)


def solution(mesh):
    return jax.shard_map(
        local,
        mesh=mesh,
        in_specs=(
            P(None, AXES),
            P(None, AXES),
            P(),
            P(),
            P(AXES, None),
            P(AXES, None),
            P(AXES),
        ),
        out_specs=P(None, AXES),
        check_vma=False,
    )
```
